128 devices in a mesh: row: 8 (over z, core), col: 16 (over x, y).
Axes of the slice: x: 4, y: 4, z: 4, core: 2. Of those that a mesh axis runs over, the one named last changes fastest.
Arguments:
- reflection: bfloat16 [2, 1024, 16384], P(None, 'col', 'row'), may hold values from -6 to 6
- focus_in: bfloat16 [2, 16384, 8192], P(None, 'row', 'col'), may hold values from -1 to 1
- focus_out: bfloat16 [2, 8192, 1024], P(None, 'row'), may hold values from -1 to 1
- ref_angle: float32 [8192, 8192], P('row', 'col'), may hold values from -3.140625 to 3.140625
- element_order: int32 [16384], P('row'), may hold values from 0 to 16383, as said below
- q_start: bfloat16 [8192, 2, 256], P('row'), may hold values from -1 to 1
Outputs:
- basis: float32 [8192, 2, 256], P(('row', 'col'))
The draws below stay inside these ranges and needn't reach their ends.
Inputs may be any that keep to these rules, and one draw needn't show every extreme that they name: `element_order`: a permutation of 0 to 16383 that maps each aligned block of 512 positions onto the same block.
All inputs are finite; a program needn't handle non-finite values.
Results may differ from the reference program's by a relative error of at most 0.0047.
Values may be sent and summed in bfloat16 or wider, within the bound.
A program may use at most 192 MiB of HBM per device.

```python
import math
import jax
import jax.numpy as jnp
from jax import lax

NF = 8192
RANK = 256
PANEL_W = 512
OUT_TRANS = 1024
IN_TRANS = 16384


def draw_element_order(key, part):
    blocks = IN_TRANS // PANEL_W
    keys = jax.random.split(jax.random.fold_in(key, 17), blocks)
    shuffled = jax.vmap(lambda single: jax.random.permutation(single, PANEL_W))(keys)
    offsets = (jnp.arange(blocks, dtype=jnp.int32) * PANEL_W)[:, None]
    return (shuffled.astype(jnp.int32) + offsets).reshape(-1).astype(jnp.int32)


def drawn_field(key, shape, scale):
    values = jax.random.truncated_normal(key, -6.0, 6.0, shape, jnp.float32)
    return (values * scale).astype(jnp.bfloat16)


def draw_reflection(key, part):
    return drawn_field(jax.random.fold_in(key, 31), (2, OUT_TRANS, IN_TRANS), 1.0)


def draw_focus_in(key, part):
    return drawn_field(jax.random.fold_in(key, 37), (2, IN_TRANS, NF), IN_TRANS ** (-0.5))


def draw_focus_out(key, part):
    return drawn_field(jax.random.fold_in(key, 41), (2, NF, OUT_TRANS), OUT_TRANS ** (-0.5))


def draw_q_start(key, part):
    return drawn_field(jax.random.fold_in(key, 43), (NF, 2, RANK), NF ** (-0.5))


def setup_inputs(seed: int = 0) -> dict:
    arg_keys = jax.random.split(jax.random.key(seed), 7)
    reflection = draw_reflection(jax.random.fold_in(arg_keys[6], 71), 0)
    focus_in = draw_focus_in(jax.random.fold_in(arg_keys[6], 71), 0)
    focus_out = draw_focus_out(jax.random.fold_in(arg_keys[6], 71), 0)
    ref_angle = jnp.clip(jax.random.uniform(arg_keys[3], (NF, NF), jnp.float32, -3.140625, 3.140625), -3.140625, 3.140625)
    element_order = draw_element_order(jax.random.fold_in(arg_keys[6], 71), 0)
    q_start = draw_q_start(jax.random.fold_in(arg_keys[6], 71), 0)
    return dict(reflection=reflection, focus_in=focus_in, focus_out=focus_out, ref_angle=ref_angle, element_order=element_order, q_start=q_start)


def cross(left_re, left_im, right_re, right_im):
    real_part = jnp.dot(left_re, right_re, preferred_element_type=jnp.float32) - jnp.dot(left_im, right_im, preferred_element_type=jnp.float32)
    imag_part = jnp.dot(left_re, right_im, preferred_element_type=jnp.float32) + jnp.dot(left_im, right_re, preferred_element_type=jnp.float32)
    return (real_part, imag_part)

def tdot(left, right, precision=None):
    return lax.dot_general(left, right, (((0,), (0,)), ((), ())), precision=precision, preferred_element_type=jnp.float32)

def adjoint_product(left_re, left_im, right_re, right_im, precision=None):
    real_part = tdot(left_re, right_re, precision) + tdot(left_im, right_im, precision)
    imag_part = tdot(left_re, right_im, precision) - tdot(left_im, right_re, precision)
    return (real_part, imag_part)

def complex_chol(gram_re, gram_im):
    order = gram_re.shape[0]
    positions = jnp.arange(order)
    high = lax.Precision.HIGHEST

    def step(column, carry):
        low_re, low_im = carry
        row_re = low_re[column]
        row_im = low_im[column]
        value_re = gram_re[:, column] - (jnp.dot(low_re, row_re, precision=high) + jnp.dot(low_im, row_im, precision=high))
        value_im = gram_im[:, column] - (jnp.dot(low_im, row_re, precision=high) - jnp.dot(low_re, row_im, precision=high))
        pivot = jnp.sqrt(value_re[column])
        below = positions > column
        new_re = jnp.where(below, value_re / pivot, jnp.where(positions == column, pivot, jnp.zeros_like(pivot)))
        new_im = jnp.where(below, value_im / pivot, jnp.zeros_like(pivot))
        return (low_re.at[:, column].set(new_re), low_im.at[:, column].set(new_im))
    start = (jnp.zeros((order, order), jnp.float32), jnp.zeros((order, order), jnp.float32))
    return lax.fori_loop(0, order, step, start)

def lower_inverse(low_re, low_im):
    order = low_re.shape[0]
    positions = jnp.arange(order)
    high = lax.Precision.HIGHEST

    def step(column, carry):
        inv_re, inv_im = carry
        row_re = low_re[column]
        row_im = low_im[column]
        sum_re = jnp.dot(row_re, inv_re, precision=high) - jnp.dot(row_im, inv_im, precision=high)
        sum_im = jnp.dot(row_re, inv_im, precision=high) + jnp.dot(row_im, inv_re, precision=high)
        pivot = low_re[column, column]
        unit = (positions == column).astype(jnp.float32)
        return (inv_re.at[column].set((unit - sum_re) / pivot), inv_im.at[column].set(-sum_im / pivot))
    start = (jnp.zeros((order, order), jnp.float32), jnp.zeros((order, order), jnp.float32))
    return lax.fori_loop(0, order, step, start)

def orthonormal(image_re, image_im, gram_re, gram_im, scale):
    high = lax.Precision.HIGHEST
    low_re, low_im = complex_chol(gram_re, gram_im)
    inv_re, inv_im = lower_inverse(low_re, low_im)
    basis_re = jnp.dot(image_re, inv_re.T, precision=high) + jnp.dot(image_im, inv_im.T, precision=high)
    basis_im = jnp.dot(image_im, inv_re.T, precision=high) - jnp.dot(image_re, inv_im.T, precision=high)
    return jnp.stack([basis_re, basis_im], axis=1) * scale

def reference(reflection, focus_in, focus_out, ref_angle, element_order, q_start):
    ordered = jnp.take(focus_in, element_order.astype(jnp.int32), axis=1)
    focus_re, focus_im = cross(reflection[0], reflection[1], ordered[0], ordered[1])
    focus_re = focus_re.astype(jnp.bfloat16)
    focus_im = focus_im.astype(jnp.bfloat16)
    outer_re, outer_im = cross(focus_out[0], focus_out[1], focus_re, focus_im)
    cosine = jnp.cos(ref_angle)
    sine = jnp.sin(ref_angle)
    dense_re = (outer_re * cosine + outer_im * sine).astype(jnp.bfloat16)
    dense_im = (outer_im * cosine - outer_re * sine).astype(jnp.bfloat16)
    adj_re, adj_im = adjoint_product(dense_re, dense_im, q_start[:, 0], q_start[:, 1])
    adj_re = adj_re.astype(jnp.bfloat16)
    adj_im = adj_im.astype(jnp.bfloat16)
    image_re, image_im = cross(dense_re, dense_im, adj_re, adj_im)
    gram_re, gram_im = adjoint_product(image_re, image_im, image_re, image_im, lax.Precision.HIGHEST)
    return orthonormal(image_re, image_im, gram_re, gram_im, math.sqrt(NF))
```

```python
import functools
import math

import jax
import jax.numpy as jnp
from jax import lax
from jax.experimental import pallas as pl
from jax.experimental.pallas import tpu as pltpu
from jax.sharding import PartitionSpec as P

NF = 8192
PANEL_W = 512
NB = 32
HI = lax.Precision.HIGHEST
RANK=256

def dott(a, b, precision=HI):
    return lax.dot_general(a, b, (((1,), (1,)), ((), ())), precision=precision, preferred_element_type=jnp.float32)

def factor_inverse(diag):
    lane = lax.broadcasted_iota(jnp.int32, (NB, 4 * NB), 1)
    sub = lax.broadcasted_iota(jnp.int32, (NB, 4 * NB), 0)
    unit = (lane - 2 * NB == sub).astype(jnp.float32)
    unit_i = (lane - 3 * NB == sub).astype(jnp.float32)
    re, im = diag[:, :NB], diag[:, NB:]
    z = jnp.zeros((NB, 2 * NB), jnp.float32)
    w = jnp.concatenate([re, im, z], axis=1) + unit
    v = jnp.concatenate([-im, re, z], axis=1) + unit_i
    sub1 = sub[:, :1]
    for j in range(NB - 1):
        piv = w[j : j + 1, j : j + 1]
        below = sub1 > j
        c_re = jnp.where(below, w[:, j : j + 1], 0.0)
        c_im = jnp.where(below, w[:, NB + j : NB + j + 1], 0.0)
        inv = 1.0 / piv
        row = w[j : j + 1, :] * inv
        rov = v[j : j + 1, :] * inv
        w = w - (c_re * row + c_im * rov)
        v = v - (c_re * rov - c_im * row)
    d = jnp.sum(jnp.where(lane == sub, w, 0.0), axis=1, keepdims=True)
    return w[:, 2 * NB :] * lax.rsqrt(d)

def swapped(m):
    return jnp.concatenate([-m[:, NB:], m[:, :NB]], axis=1)

def chol_kernel(scale, g_ref, y_ref, out_ref, a_ref):
    n = RANK
    rows = y_ref.shape[0]
    panels = n // NB
    a_ref[:n, :] = g_ref[...]
    a_ref[n:, :] = y_ref[...]
    for k in range(panels):
        lo = k * NB
        inv = factor_inverse(a_ref[lo : lo + NB, 2 * lo : 2 * lo + 2 * NB])
        both = jnp.concatenate([inv, swapped(inv)], axis=0)
        ap = a_ref[lo + NB :, 2 * lo : 2 * lo + 2 * NB]
        low = dott(ap, both)
        x = low[low.shape[0] - rows :] * scale
        out_ref[:, 0, lo : lo + NB] = x[:, :NB]
        out_ref[:, 1, lo : lo + NB] = x[:, NB:]
        left = panels - 1 - k
        if left:
            lk = low[: left * NB]
            sk = swapped(lk)
            q = jnp.concatenate([lk.reshape(left, NB, 2 * NB), sk.reshape(left, NB, 2 * NB)], axis=1)
            q = q.reshape(left * 2 * NB, 2 * NB)
            a_ref[lo + NB :, 2 * lo + 2 * NB :] -= dott(low, q)

def chol(g, y, scale):
    return pl.pallas_call(
        functools.partial(chol_kernel, scale),
        out_shape=jax.ShapeDtypeStruct((y.shape[0], 2, RANK), jnp.float32),
        in_specs=[pl.BlockSpec(memory_space=pltpu.VMEM)] * 2,
        out_specs=pl.BlockSpec(memory_space=pltpu.VMEM),
        scratch_shapes=[pltpu.VMEM((RANK + y.shape[0], 2 * RANK), jnp.float32)],
    )(g, y)

def interleave(re, im):
    r = re.shape[0]
    return jnp.stack([re.reshape(r, -1, NB), im.reshape(r, -1, NB)], axis=2).reshape(r, -1)


def times_i(m):
    r = m.shape[0]
    pairs = m.reshape(r, -1, 2, NB)
    return jnp.stack([-pairs[:, :, 1], pairs[:, :, 0]], axis=2).reshape(r, -1)


def f32dot(a, b, dims, precision=None):
    return lax.dot_general(a, b, ((dims[0], dims[1]), ((), ())), precision=precision, preferred_element_type=jnp.float32)


def body(reflection, focus_in, focus_out, ref_angle, element_order, q_start):
    local_inputs = focus_in.shape[1]
    blocks = local_inputs // PANEL_W
    place = (element_order % PANEL_W).reshape(blocks, PANEL_W)
    onehot = (place[:, :, None] == jnp.arange(PANEL_W, dtype=jnp.int32)).astype(jnp.bfloat16)
    refl = reflection.reshape(2 * reflection.shape[1], blocks, PANEL_W)
    refl = jnp.einsum("mbt,bts->mbs", refl, onehot, preferred_element_type=jnp.float32).astype(jnp.bfloat16)
    refl = refl.reshape(reflection.shape)
    piece = lax.all_gather(refl, "col", axis=1, tiled=True)
    part_re = f32dot(piece[0], focus_in[0], ((1,), (0,))) - f32dot(piece[1], focus_in[1], ((1,), (0,)))
    part_im = f32dot(piece[0], focus_in[1], ((1,), (0,))) + f32dot(piece[1], focus_in[0], ((1,), (0,)))
    focused = lax.psum(jnp.stack([part_re, part_im]), "row").astype(jnp.bfloat16)
    outer_re = f32dot(focus_out[0], focused[0], ((1,), (0,))) - f32dot(focus_out[1], focused[1], ((1,), (0,)))
    outer_im = f32dot(focus_out[0], focused[1], ((1,), (0,))) + f32dot(focus_out[1], focused[0], ((1,), (0,)))
    cosine = jnp.cos(ref_angle)
    sine = jnp.sin(ref_angle)
    dense_re = (outer_re * cosine + outer_im * sine).astype(jnp.bfloat16)
    dense_im = (outer_im * cosine - outer_re * sine).astype(jnp.bfloat16)
    q1 = interleave(q_start[:, 0], q_start[:, 1])
    q2 = interleave(q_start[:, 1], -q_start[:, 0])
    adj = f32dot(dense_re, q1, ((0,), (0,))) + f32dot(dense_im, q2, ((0,), (0,)))
    adj = lax.psum(adj, "row").astype(jnp.bfloat16)
    image = f32dot(dense_re, adj, ((1,), (0,))) + f32dot(dense_im, times_i(adj), ((1,), (0,)))
    image = lax.psum_scatter(image, "col", scatter_dimension=0, tiled=True)
    im_re = image.reshape(-1, RANK // NB, 2, NB)[:, :, 0].reshape(-1, RANK)
    im_im = image.reshape(-1, RANK // NB, 2, NB)[:, :, 1].reshape(-1, RANK)
    gram = f32dot(im_re, image, ((0,), (0,)), HI) - f32dot(im_im, times_i(image), ((0,), (0,)), HI)
    gram = lax.psum(gram, ("row", "col"))
    return chol(gram, image, math.sqrt(NF))


def solution(mesh):
    in_specs = (
        P(None, "col", "row"),
        P(None, "row", "col"),
        P(None, "row", None),
        P("row", "col"),
        P("row"),
        P("row", None, None),
    )
    out_specs = P(("row", "col"), None, None)
    return jax.shard_map(body, mesh=mesh, in_specs=in_specs, out_specs=out_specs, check_vma=False)
```

```python
import functools
import math

import jax
import jax.numpy as jnp
from jax import lax
from jax.experimental import pallas as pl
from jax.experimental.pallas import tpu as pltpu
from jax.sharding import PartitionSpec as P

NF = 8192
RANK = 256
PANEL_W = 512
NB = 32
HI = lax.Precision.HIGHEST
MESH = pl.DeviceIdType.MESH


def dot_nt(a, b, precision=None):
    return lax.dot_general(a, b, (((1,), (1,)), ((), ())), precision=precision, preferred_element_type=jnp.float32)


def dot_nn(a, b):
    return jnp.dot(a, b, preferred_element_type=jnp.float32)


def dot_tn(a, b, precision=None):
    return lax.dot_general(a, b, (((0,), (0,)), ((), ())), precision=precision, preferred_element_type=jnp.float32)


def remote(src, dst, send_sem, recv_sem, row, col):
    return pltpu.make_async_remote_copy(
        src_ref=src, dst_ref=dst, send_sem=send_sem, recv_sem=recv_sem, device_id=(row, col), device_id_type=MESH
    )


def tail_kernel(
    dense_re, dense_im, qt_ref, image_ref, gram_ref,
    zpart, zs1, zr1, zs2, zr2, zfull,
    yown_a, yown_b, ysa, ysb, yra, yrb, ys2, yr2a, yr2b,
    hpart, hrecv, hrow,
    sz1, rz1, sz2, rz2, sz3, rz3, sz4, rz4, sya, rya, syb, ryb, sy2a, ry2a, sy2b, ry2b, sh1, rh1, sh2, rh2, sh3, rh3,
):
    r = lax.axis_index("row")
    c = lax.axis_index("col")
    z, core = r // 2, r % 2
    x, y = c // 4, c % 4
    other = 1 - core

    barrier = pltpu.get_barrier_semaphore()
    for d in range(1, 8):
        pl.semaphore_signal(barrier, inc=1, device_id=((r + d) % 8, c), device_id_type=MESH)
    for d in range(1, 16):
        pl.semaphore_signal(barrier, inc=1, device_id=(r, (c + d) % 16), device_id_type=MESH)

    half = RANK
    q1 = qt_ref[...]
    q2 = jnp.concatenate([q1[half:], -q1[:half]], axis=0)
    zpart[...] = dot_nn(q1, dense_re[...]) + dot_nn(q2, dense_im[...])
    pl.semaphore_wait(barrier, 22)
    zs1[...] = zpart[pl.ds(other * half, half), :].astype(zs1.dtype)
    pair = remote(zs1, zr1, sz1, rz1, z * 2 + other, c)
    pair.start()
    pair.wait_recv()
    mine = zpart[pl.ds(core * half, half), :] + zr1[...].astype(jnp.float32)
    quarter = half // 4
    zs2[...] = mine.reshape(4, quarter, -1).astype(zs2.dtype)
    zpart[pl.ds(0, half), :] = mine
    sends = []
    for d in range(1, 4):
        to = (z + d) % 4
        sends.append(remote(zs2.at[to], zr2.at[d - 1], sz2.at[d - 1], rz2.at[d - 1], to * 2 + core, c))
        sends[-1].start()
    total = zpart[pl.ds(z * quarter, quarter), :]
    for d in range(1, 4):
        sends[d - 1].wait_recv()
        total = total + zr2[d - 1].astype(jnp.float32)
    slot = core * half + z * quarter
    own = zfull.at[pl.ds(slot, quarter), :]
    zfull[pl.ds(slot, quarter), :] = total.astype(jnp.bfloat16)
    spread = []
    for d in range(1, 4):
        to = (z + d) % 4
        spread.append(remote(own, own, sz3.at[d - 1], rz3.at[d - 1], to * 2 + core, c))
        spread[-1].start()
    relay = [remote(own, own, sz4.at[0], rz4.at[0], z * 2 + other, c)]
    relay[0].start()
    for d in range(1, 4):
        spread[d - 1].wait_recv()
        origin = (z + 4 - d) % 4
        part = zfull.at[pl.ds(core * half + origin * quarter, quarter), :]
        relay.append(remote(part, part, sz4.at[d], rz4.at[d], z * 2 + other, c))
        relay[-1].start()
    for d in range(4):
        relay[d].wait_recv()

    z1 = zfull[...]
    z2 = jnp.concatenate([-z1[half:], z1[:half]], axis=0)
    first_a = []
    for d in (1, 2, 3, 0):
        to = (x + d) % 4
        rows = pl.ds(to * 256, 256)
        block = dot_nt(dense_re[rows, :], z1) + dot_nt(dense_im[rows, :], z2)
        block_a = block[:, :half].reshape(4, 64, half)
        block_b = block[:, half:].reshape(4, 64, half)
        for j in range(4):
            ysb[j, to] = block_b[j].astype(ysb.dtype)
            yown_b[j, to] = block_b[j]
        if d:
            ysa[d - 1] = block_a.astype(ysa.dtype)
            first_a.append(remote(ysa.at[d - 1], yra.at[d - 1], sya.at[d - 1], rya.at[d - 1], r, to * 4 + y))
            first_a[-1].start()
        else:
            yown_a[...] = block_a
    first_b = []
    for d in range(1, 4):
        to = (y + d) % 4
        first_b.append(remote(ysb.at[to], yrb.at[d - 1], syb.at[d - 1], ryb.at[d - 1], r, x * 4 + to))
        first_b[-1].start()
    sum_a = yown_a[...]
    for d in range(1, 4):
        first_a[d - 1].wait_recv()
        sum_a = sum_a + yra[d - 1].astype(jnp.float32)
    yown_a[...] = sum_a
    ys2[0] = sum_a.astype(ys2.dtype)
    second_a = []
    for d in range(1, 4):
        to = (y + d) % 4
        second_a.append(remote(ys2.at[0, to], yr2a.at[d - 1], sy2a.at[d - 1], ry2a.at[d - 1], r, x * 4 + to))
        second_a[-1].start()
    sum_b = yown_b[y]
    for d in range(1, 4):
        first_b[d - 1].wait_recv()
        sum_b = sum_b + yrb[d - 1].astype(jnp.float32)
    yown_b[0] = sum_b
    ys2[1] = sum_b.astype(ys2.dtype)
    second_b = []
    for d in range(1, 4):
        to = (x + d) % 4
        second_b.append(remote(ys2.at[1, to], yr2b.at[d - 1], sy2b.at[d - 1], ry2b.at[d - 1], r, to * 4 + y))
        second_b[-1].start()
    final_a = yown_a[y]
    for d in range(1, 4):
        second_a[d - 1].wait_recv()
        final_a = final_a + yr2a[d - 1].astype(jnp.float32)
    final_b = yown_b[0, x]
    for d in range(1, 4):
        second_b[d - 1].wait_recv()
        final_b = final_b + yr2b[d - 1].astype(jnp.float32)
    image_ref[:, :half] = final_a
    image_ref[:, half:] = final_b

    both = jnp.concatenate([final_a, final_b], axis=0)
    turned = jnp.concatenate([final_b, -final_a], axis=0)
    gram_re = dot_tn(both, both, HI)
    gram_im = dot_tn(both, turned, HI)
    rows = lax.broadcasted_iota(jnp.int32, (RANK, RANK), 0)
    cols = lax.broadcasted_iota(jnp.int32, (RANK, RANK), 1)
    hpart[...] = jnp.where(rows >= cols, gram_re, gram_im).reshape(16, 16, RANK)
    g1 = []
    for d in range(1, 16):
        to = (c + d) % 16
        g1.append(remote(hpart.at[to], hrecv.at[d - 1], sh1.at[d - 1], rh1.at[d - 1], r, to))
        g1[-1].start()
    acc = hpart[c]
    for d in range(1, 16):
        g1[d - 1].wait_recv()
        acc = acc + hrecv[d - 1]
    hrow[r] = acc
    g2 = []
    for d in range(1, 8):
        g2.append(remote(hrow.at[r], hrow.at[r], sh2.at[d - 1], rh2.at[d - 1], (r + d) % 8, c))
        g2[-1].start()
    for d in range(1, 8):
        g2[d - 1].wait_recv()
    acc = hrow[0]
    for i in range(1, 8):
        acc = acc + hrow[i]
    gram_ref[c] = acc
    g3 = []
    for d in range(1, 16):
        g3.append(remote(gram_ref.at[c], gram_ref.at[c], sh3.at[d - 1], rh3.at[d - 1], r, (c + d) % 16))
        g3[-1].start()
    for d in range(1, 16):
        g3[d - 1].wait_recv()
    for copy in [pair] + sends + spread + relay + first_a + first_b + second_a + second_b + g1 + g2 + g3:
        copy.wait_send()


def tail(dense_re, dense_im, qt):
    bf, f32 = jnp.bfloat16, jnp.float32
    dma = pltpu.SemaphoreType.DMA
    vm = pltpu.VMEM
    scratch = [
        vm((512, 512), f32), vm((256, 512), bf), vm((256, 512), bf), vm((4, 64, 512), bf), vm((3, 64, 512), bf), vm((512, 512), bf),
        vm((4, 64, 256), f32), vm((4, 4, 64, 256), f32), vm((3, 4, 64, 256), bf), vm((4, 4, 64, 256), bf),
        vm((3, 4, 64, 256), bf), vm((3, 4, 64, 256), bf), vm((2, 4, 64, 256), f32), vm((3, 64, 256), f32), vm((3, 64, 256), f32),
        vm((16, 16, RANK), f32), vm((15, 16, RANK), f32), vm((8, 16, RANK), f32),
        dma, dma, dma((3,)), dma((3,)), dma((3,)), dma((3,)), dma((4,)), dma((4,)), dma((3,)), dma((3,)), dma((3,)), dma((3,)),
        dma((3,)), dma((3,)), dma((3,)), dma((3,)), dma((15,)), dma((15,)), dma((7,)), dma((7,)), dma((15,)), dma((15,)),
    ]
    vmem = pl.BlockSpec(memory_space=pltpu.VMEM)
    return pl.pallas_call(
        tail_kernel,
        out_shape=(jax.ShapeDtypeStruct((64, 2 * RANK), f32), jax.ShapeDtypeStruct((16, 16, RANK), f32)),
        in_specs=[vmem] * 3,
        out_specs=(vmem, vmem),
        scratch_shapes=scratch,
        compiler_params=pltpu.CompilerParams(collective_id=1, has_side_effects=True, vmem_limit_bytes=48 << 20),
    )(dense_re, dense_im, qt)


def factor_inverse(diag):
    lane = lax.broadcasted_iota(jnp.int32, (NB, 4 * NB), 1)
    sub = lax.broadcasted_iota(jnp.int32, (NB, 4 * NB), 0)
    unit = (lane - 2 * NB == sub).astype(jnp.float32)
    unit_i = (lane - 3 * NB == sub).astype(jnp.float32)
    re, im = diag[:, :NB], diag[:, NB:]
    z = jnp.zeros((NB, 2 * NB), jnp.float32)
    w = jnp.concatenate([re, im, z], axis=1) + unit
    v = jnp.concatenate([-im, re, z], axis=1) + unit_i
    sub1 = sub[:, :1]
    for j in range(NB - 1):
        piv = w[j : j + 1, j : j + 1]
        below = sub1 > j
        c_re = jnp.where(below, w[:, j : j + 1], 0.0)
        c_im = jnp.where(below, w[:, NB + j : NB + j + 1], 0.0)
        inv = 1.0 / piv
        row = w[j : j + 1, :] * inv
        rov = v[j : j + 1, :] * inv
        w = w - (c_re * row + c_im * rov)
        v = v - (c_re * rov - c_im * row)
    d = jnp.sum(jnp.where(lane == sub, w, 0.0), axis=1, keepdims=True)
    return w[:, 2 * NB :] * lax.rsqrt(d)


def swapped(m):
    return jnp.concatenate([-m[:, NB:], m[:, :NB]], axis=1)


def chol_kernel(scale, g_ref, y_ref, out_ref, a_ref):
    n = RANK
    rows = y_ref.shape[0]
    panels = n // NB
    packed = g_ref[...]
    turned = packed.T
    sub = lax.broadcasted_iota(jnp.int32, (n, n), 0)
    lane = lax.broadcasted_iota(jnp.int32, (n, n), 1)
    g_re = jnp.where(sub >= lane, packed, turned)
    g_im = jnp.where(sub > lane, -turned, jnp.where(sub == lane, 0.0, packed))
    for k in range(panels):
        a_ref[:n, 2 * NB * k : 2 * NB * k + NB] = g_re[:, NB * k : NB * k + NB]
        a_ref[:n, 2 * NB * k + NB : 2 * NB * (k + 1)] = g_im[:, NB * k : NB * k + NB]
        a_ref[n:, 2 * NB * k : 2 * NB * k + NB] = y_ref[:, NB * k : NB * k + NB]
        a_ref[n:, 2 * NB * k + NB : 2 * NB * (k + 1)] = y_ref[:, n + NB * k : n + NB * k + NB]
    for k in range(panels):
        lo = k * NB
        inv = factor_inverse(a_ref[lo : lo + NB, 2 * lo : 2 * lo + 2 * NB])
        both = jnp.concatenate([inv, swapped(inv)], axis=0)
        ap = a_ref[lo + NB :, 2 * lo : 2 * lo + 2 * NB]
        low = dot_nt(ap, both, HI)
        solved = low[low.shape[0] - rows :] * scale
        out_ref[:, 0, lo : lo + NB] = solved[:, :NB]
        out_ref[:, 1, lo : lo + NB] = solved[:, NB:]
        left = panels - 1 - k
        if left:
            lk = low[: left * NB]
            q = jnp.concatenate([lk.reshape(left, NB, 2 * NB), swapped(lk).reshape(left, NB, 2 * NB)], axis=1)
            q = q.reshape(left * 2 * NB, 2 * NB)
            a_ref[lo + NB :, 2 * lo + 2 * NB :] -= dot_nt(low, q, HI)


def chol(g, y, scale):
    vmem = pl.BlockSpec(memory_space=pltpu.VMEM)
    return pl.pallas_call(
        functools.partial(chol_kernel, scale),
        out_shape=jax.ShapeDtypeStruct((y.shape[0], 2, RANK), jnp.float32),
        in_specs=[vmem] * 2,
        out_specs=vmem,
        scratch_shapes=[pltpu.VMEM((RANK + y.shape[0], 2 * RANK), jnp.float32)],
    )(g, y)


def f32dot(a, b, dims, precision=None):
    return lax.dot_general(a, b, ((dims[0], dims[1]), ((), ())), precision=precision, preferred_element_type=jnp.float32)


def body(reflection, focus_in, focus_out, ref_angle, element_order, q_start):
    local_inputs = focus_in.shape[1]
    blocks = local_inputs // PANEL_W
    place = (element_order % PANEL_W).reshape(blocks, PANEL_W)
    onehot = (place[:, :, None] == jnp.arange(PANEL_W, dtype=jnp.int32)).astype(jnp.bfloat16)
    refl = reflection.reshape(2 * reflection.shape[1], blocks, PANEL_W)
    refl = jnp.einsum("mbt,bts->mbs", refl, onehot, preferred_element_type=jnp.float32).astype(jnp.bfloat16)
    refl = refl.reshape(reflection.shape)
    piece = lax.all_gather(refl, "col", axis=1, tiled=True)
    part_re = f32dot(piece[0], focus_in[0], ((1,), (0,))) - f32dot(piece[1], focus_in[1], ((1,), (0,)))
    part_im = f32dot(piece[0], focus_in[1], ((1,), (0,))) + f32dot(piece[1], focus_in[0], ((1,), (0,)))
    focused = lax.psum(jnp.stack([part_re, part_im]), "row").astype(jnp.bfloat16)
    outer_re = f32dot(focus_out[0], focused[0], ((1,), (0,))) - f32dot(focus_out[1], focused[1], ((1,), (0,)))
    outer_im = f32dot(focus_out[0], focused[1], ((1,), (0,))) + f32dot(focus_out[1], focused[0], ((1,), (0,)))
    cosine = jnp.cos(ref_angle)
    sine = jnp.sin(ref_angle)
    dense_re = (outer_re * cosine + outer_im * sine).astype(jnp.bfloat16)
    dense_im = (outer_im * cosine - outer_re * sine).astype(jnp.bfloat16)
    qt = jnp.transpose(q_start, (1, 2, 0)).reshape(2 * RANK, -1)
    image, gram = tail(dense_re, dense_im, qt)
    return chol(gram.reshape(RANK, RANK), image, math.sqrt(NF))


def solution(mesh):
    in_specs = (
        P(None, "col", "row"),
        P(None, "row", "col"),
        P(None, "row", None),
        P("row", "col"),
        P("row"),
        P("row", None, None),
    )
    out_specs = P(("row", "col"), None, None)
    return jax.shard_map(body, mesh=mesh, in_specs=in_specs, out_specs=out_specs, check_vma=False)
```

```python
import functools
import math

import jax
import jax.numpy as jnp
from jax import lax
from jax.experimental import pallas as pl
from jax.experimental.pallas import tpu as pltpu
from jax.sharding import PartitionSpec as P

NF = 8192
RANK = 256
PANEL_W = 512
NB = 32
HI = lax.Precision.HIGHEST
MESH = pl.DeviceIdType.MESH


def dot_nt(a, b, precision=None):
    return lax.dot_general(a, b, (((1,), (1,)), ((), ())), precision=precision, preferred_element_type=jnp.float32)


def dot_nn(a, b):
    return jnp.dot(a, b, preferred_element_type=jnp.float32)


def dot_tn(a, b, precision=None):
    return lax.dot_general(a, b, (((0,), (0,)), ((), ())), precision=precision, preferred_element_type=jnp.float32)


def remote(src, dst, send_sem, recv_sem, row, col):
    return pltpu.make_async_remote_copy(
        src_ref=src, dst_ref=dst, send_sem=send_sem, recv_sem=recv_sem, device_id=(row, col), device_id_type=MESH
    )


def cos_sin(angle):
    half = 0.5 * angle
    t = half * half
    s = -1.0 / 39916800.0
    for k in (1.0 / 362880.0, -1.0 / 5040.0, 1.0 / 120.0, -1.0 / 6.0, 1.0):
        s = s * t + k
    s = s * half
    c = 1.0 / 479001600.0
    for k in (-1.0 / 3628800.0, 1.0 / 40320.0, -1.0 / 720.0, 1.0 / 24.0, -0.5, 1.0):
        c = c * t + k
    return 1.0 - 2.0 * s * s, 2.0 * s * c


def head_kernel(
    refl_ref, order_ref, focus_in_hbm, focus_out_hbm, angle_hbm, dense_re, dense_im,
    gat, p_ref, f_ref, angle, cpart, crecv, zsend, zrecv, cfull,
    local_sem, gs, gr, ps, pr, zs, zr, cs, cr, ws, wr,
):
    r = lax.axis_index("row")
    c = lax.axis_index("col")
    z, core = r // 2, r % 2
    x, y = c // 4, c % 4
    other = 1 - core
    up = {"x": (x + 1) % 4, "y": (y + 1) % 4}
    down = {"x": (x + 3) % 4, "y": (y + 3) % 4}
    far_x, far_y = (x + 2) % 4, (y + 2) % 4
    left, right, low, high = down["x"], up["x"], down["y"], up["y"]

    loads = [
        pltpu.make_async_copy(focus_in_hbm, p_ref, local_sem.at[0]),
        pltpu.make_async_copy(focus_out_hbm, f_ref, local_sem.at[1]),
        pltpu.make_async_copy(angle_hbm, angle, local_sem.at[2]),
    ]
    for copy in loads:
        copy.start()
    barrier = pltpu.get_barrier_semaphore()
    for to in ((r, right * 4 + y), (r, left * 4 + y), (r, x * 4 + high), (r, x * 4 + low), (z * 2 + other, c)):
        pl.semaphore_signal(barrier, inc=1, device_id=to, device_id_type=MESH)
    for d in range(1, 4):
        pl.semaphore_signal(barrier, inc=1, device_id=((z + d) % 4 * 2 + core, c), device_id_type=MESH)

    sub = lax.broadcasted_iota(jnp.int32, (PANEL_W, PANEL_W), 0)
    for b in range(refl_ref.shape[2] // PANEL_W):
        lanes = pl.ds(b * PANEL_W, PANEL_W)
        place = order_ref[:, lanes] & (PANEL_W - 1)
        onehot = jnp.where(place == sub, 1.0, 0.0).astype(jnp.bfloat16)
        raw = jnp.concatenate([refl_ref[0, :32, lanes], refl_ref[1, :32, lanes], refl_ref[0, 32:, lanes], refl_ref[1, 32:, lanes]], axis=0)
        moved = dot_nt(raw, onehot).astype(jnp.bfloat16)
        gat[x, y, 0, :, lanes] = moved[:64]
        gat[x, y, 1, :, lanes] = moved[64:]
    pl.semaphore_wait(barrier, 8)

    copies = {}

    def send(name, sx, sy, h, piece=None):
        axis, way = name[-2], name[-1]
        to = (up if way == "+" else down)[axis]
        col = to * 4 + y if axis == "x" else x * 4 + to
        ref = gat.at[sx, sy, h] if piece is None else gat.at[sx, sy, h, pl.ds(32 * piece, 32)]
        i = len(copies)
        copies[name] = remote(ref, ref, gs.at[i], gr.at[i], r, col)
        copies[name].start()

    def got(*names):
        for name in names:
            copies[name + "+"].wait_recv()
            copies[name + "-"].wait_recv()

    def both(name, sx, sy, h):
        send(name + "+", sx, sy, h)
        send(name + "-", sx, sy, h)

    def gemm(s, parts):
        @pl.loop(0, 2)
        def _(n):
            lanes = pl.ds(pl.multiple_of(n * 256, 256), 256)
            rows = jnp.concatenate([gat[sx, sy, h] for sx, sy, h in parts], axis=0)
            by_re = dot_nn(rows, p_ref[0, :, lanes]).reshape(4, 2, 32, 256)
            by_im = dot_nn(rows, p_ref[1, :, lanes]).reshape(4, 2, 32, 256)
            cpart[s, 0, :, :, lanes] = by_re[:, 0] - by_im[:, 1]
            cpart[s, 1, :, :, lanes] = by_im[:, 0] + by_re[:, 1]

    pair, across, back, relay = {}, {}, {}, {}

    def start_pair(s):
        pair[s] = remote(cpart.at[s, other], crecv.at[s], ps.at[s], pr.at[s], z * 2 + other, c)
        pair[s].start()

    def start_across(s):
        pair[s].wait_recv()
        zsend[s] = cpart[s, core] + crecv[s]
        across[s] = []
        for d in range(1, 4):
            to = (z + d) % 4
            across[s].append(remote(zsend.at[s, to], zrecv.at[s, d - 1], zs.at[s, d - 1], zr.at[s, d - 1], to * 2 + core, c))
            across[s][-1].start()

    def place_of(parts, q):
        first = jnp.int32(0)
        for i, (sx, sy, h) in enumerate(parts):
            first = first + jnp.where(q == i, 1, 0) * (sx * 256 + sy * 64 + h * 32)
        return pl.multiple_of(first, 32)

    def start_back(s, parts):
        total = zsend[s, z]
        for d in range(1, 4):
            across[s][d - 1].wait_recv()
            total = total + zrecv[s, d - 1]
        mine = pl.ds(place_of(parts, z), 32)
        cfull[core, mine, :] = total.astype(jnp.bfloat16)
        ref = cfull.at[core, mine, :]
        back[s] = []
        for d in range(1, 4):
            back[s].append(remote(ref, ref, cs.at[s, d - 1], cr.at[s, d - 1], (z + d) % 4 * 2 + core, c))
            back[s][-1].start()
        relay[s] = [remote(ref, ref, ws.at[s, 0], wr.at[s, 0], z * 2 + other, c)]
        relay[s][0].start()

    def start_relay(s, parts):
        for d in range(1, 4):
            back[s][d - 1].wait_recv()
            ref = cfull.at[core, pl.ds(place_of(parts, (z + 4 - d) % 4), 32), :]
            relay[s].append(remote(ref, ref, ws.at[s, d], wr.at[s, d], z * 2 + other, c))
            relay[s][-1].start()

    def finish(s):
        for copy in relay[s]:
            copy.wait_recv()

    batches = [
        [(x, y, 0), (x, y, 1), (left, y, 0), (right, y, 0)],
        [(x, low, 1), (x, high, 1), (x, low, 0), (x, high, 0)],
        [(left, y, 1), (right, y, 1), (x, far_y, 1), (far_x, y, 0)],
        [(left, low, 0), (left, high, 0), (left, low, 1), (right, low, 1)],
        [(right, low, 0), (right, high, 0), (left, high, 1), (right, high, 1)],
        [(x, far_y, 0), (far_x, y, 1), (far_x, low, 0), (far_x, high, 0)],
        [(left, far_y, 1), (right, far_y, 1), (left, far_y, 0), (far_x, low, 1)],
        [(right, far_y, 0), (far_x, high, 1), (far_x, far_y, 0), (far_x, far_y, 1)],
    ]

    def progress(s):
        if 0 <= s - 1 < 8:
            start_across(s - 1)
        if 0 <= s - 2 < 8:
            start_back(s - 2, batches[s - 2])
        if 0 <= s - 3 < 8:
            start_relay(s - 3, batches[s - 3])
        if 0 <= s - 4 < 8:
            finish(s - 4)

    both("Ax", x, y, 0)
    both("By", x, y, 1)
    both("Ay", x, y, 0)
    both("Bx", x, y, 1)
    loads[0].wait()
    for s in range(8):
        if s == 0:
            got("Ax")
            send("Aqx+", left, y, 0, 0)
            send("Aqx-", right, y, 0, 1)
            got("By")
            send("Bqy+", x, low, 1, 0)
            send("Bqy-", x, high, 1, 1)
            both("A1y", left, y, 0)
            both("B1x", x, low, 1)
            both("A2y", right, y, 0)
            both("B2x", x, high, 1)
        elif s == 1:
            got("Ay")
            send("Aq0y+", x, low, 0, 0)
            send("Aq0y-", x, high, 0, 1)
            got("Bx")
            send("Bq0x+", left, y, 1, 0)
            send("Bq0x-", right, y, 1, 1)
        elif s == 2:
            got("Aqx")
            both("A3y", far_x, y, 0)
            got("Bqy")
            both("B3x", x, far_y, 1)
        elif s == 3:
            got("A1y")
            send("Aq1y+", left, low, 0, 0)
            send("Aq1y-", left, high, 0, 1)
            got("B1x")
            send("Bq1x+", left, low, 1, 0)
            send("Bq1x-", right, low, 1, 1)
        elif s == 4:
            got("A2y")
            send("Aq2y+", right, low, 0, 0)
            send("Aq2y-", right, high, 0, 1)
            got("B2x")
            send("Bq2x+", left, high, 1, 0)
            send("Bq2x-", right, high, 1, 1)
        elif s == 5:
            got("Aq0y", "Bq0x", "A3y")
            send("Aq3y+", far_x, low, 0, 0)
            send("Aq3y-", far_x, high, 0, 1)
            got("B3x")
            send("Bq3x+", left, far_y, 1, 0)
            send("Bq3x-", right, far_y, 1, 1)
        elif s == 6:
            got("Aq1y", "Bq1x")
        else:
            got("Aq2y", "Bq2x", "Aq3y", "Bq3x")
        progress(s)
        gemm(s, batches[s])
        start_pair(s)
    for s in range(8, 12):
        progress(s)

    loads[1].wait()
    loads[2].wait()

    @pl.loop(0, 8)
    def _(m):
        rows = pl.ds(pl.multiple_of(m * 128, 128), 128)
        f_re, f_im = f_ref[0, rows, :], f_ref[1, rows, :]
        outer_re = dot_nn(f_re, cfull[0]) - dot_nn(f_im, cfull[1])
        outer_im = dot_nn(f_re, cfull[1]) + dot_nn(f_im, cfull[0])
        cosine, sine = cos_sin(angle[rows, :])
        dense_re[rows, :] = (outer_re * cosine + outer_im * sine).astype(jnp.bfloat16)
        dense_im[rows, :] = (outer_im * cosine - outer_re * sine).astype(jnp.bfloat16)

    for copy in list(copies.values()) + [pair[s] for s in range(8)]:
        copy.wait_send()
    for s in range(8):
        for copy in across[s] + back[s] + relay[s]:
            copy.wait_send()


def head(reflection, order, focus_in, focus_out, ref_angle):
    bf, f32 = jnp.bfloat16, jnp.float32
    vm, dma = pltpu.VMEM, pltpu.SemaphoreType.DMA
    vmem = pl.BlockSpec(memory_space=pltpu.VMEM)
    anywhere = pl.BlockSpec(memory_space=pl.ANY)
    scratch = [
        vm((4, 4, 2, 64, 2048), bf), vm((2, 2048, 512), bf), vm((2, 1024, 1024), bf), vm((1024, 512), f32),
        vm((8, 2, 4, 32, 512), f32), vm((8, 4, 32, 512), f32), vm((8, 4, 32, 512), f32), vm((8, 3, 32, 512), f32), vm((2, 1024, 512), bf),
        dma((3,)), dma((40,)), dma((40,)), dma((8,)), dma((8,)), dma((8, 3)), dma((8, 3)), dma((8, 3)), dma((8, 3)), dma((8, 4)), dma((8, 4)),
    ]
    return pl.pallas_call(
        head_kernel,
        out_shape=(jax.ShapeDtypeStruct((1024, 512), bf), jax.ShapeDtypeStruct((1024, 512), bf)),
        in_specs=[vmem, vmem, anywhere, anywhere, anywhere],
        out_specs=(vmem, vmem),
        scratch_shapes=scratch,
        compiler_params=pltpu.CompilerParams(collective_id=0, has_side_effects=True, vmem_limit_bytes=56 << 20),
    )(reflection, order, focus_in, focus_out, ref_angle)


def tail_kernel(
    dense_re, dense_im, qt_ref, image_ref, gram_ref,
    zpart, zs1, zr1, zs2, zr2, zfull,
    yown_a, yown_b, ysa, ysb, yra, yrb, ys2, yr2a, yr2b,
    hpart, hrecv, hrow,
    sz1, rz1, sz2, rz2, sz3, rz3, sz4, rz4, sya, rya, syb, ryb, sy2a, ry2a, sy2b, ry2b, sh1, rh1, sh2, rh2, sh3, rh3,
):
    r = lax.axis_index("row")
    c = lax.axis_index("col")
    z, core = r // 2, r % 2
    x, y = c // 4, c % 4
    other = 1 - core

    barrier = pltpu.get_barrier_semaphore()
    for d in range(1, 8):
        pl.semaphore_signal(barrier, inc=1, device_id=((r + d) % 8, c), device_id_type=MESH)
    for d in range(1, 16):
        pl.semaphore_signal(barrier, inc=1, device_id=(r, (c + d) % 16), device_id_type=MESH)

    half = RANK
    q1 = qt_ref[...]
    q2 = jnp.concatenate([q1[half:], -q1[:half]], axis=0)
    zpart[...] = dot_nn(q1, dense_re[...]) + dot_nn(q2, dense_im[...])
    pl.semaphore_wait(barrier, 22)
    zs1[...] = zpart[pl.ds(other * half, half), :].astype(zs1.dtype)
    pair = remote(zs1, zr1, sz1, rz1, z * 2 + other, c)
    pair.start()
    pair.wait_recv()
    mine = zpart[pl.ds(core * half, half), :] + zr1[...].astype(jnp.float32)
    quarter = half // 4
    zs2[...] = mine.reshape(4, quarter, -1).astype(zs2.dtype)
    zpart[pl.ds(0, half), :] = mine
    sends = []
    for d in range(1, 4):
        to = (z + d) % 4
        sends.append(remote(zs2.at[to], zr2.at[d - 1], sz2.at[d - 1], rz2.at[d - 1], to * 2 + core, c))
        sends[-1].start()
    total = zpart[pl.ds(z * quarter, quarter), :]
    for d in range(1, 4):
        sends[d - 1].wait_recv()
        total = total + zr2[d - 1].astype(jnp.float32)
    slot = core * half + z * quarter
    own = zfull.at[pl.ds(slot, quarter), :]
    zfull[pl.ds(slot, quarter), :] = total.astype(jnp.bfloat16)
    spread = []
    for d in range(1, 4):
        to = (z + d) % 4
        spread.append(remote(own, own, sz3.at[d - 1], rz3.at[d - 1], to * 2 + core, c))
        spread[-1].start()
    relay = [remote(own, own, sz4.at[0], rz4.at[0], z * 2 + other, c)]
    relay[0].start()
    for d in range(1, 4):
        spread[d - 1].wait_recv()
        origin = (z + 4 - d) % 4
        part = zfull.at[pl.ds(core * half + origin * quarter, quarter), :]
        relay.append(remote(part, part, sz4.at[d], rz4.at[d], z * 2 + other, c))
        relay[-1].start()
    for d in range(4):
        relay[d].wait_recv()

    z1 = zfull[...]
    z2 = jnp.concatenate([-z1[half:], z1[:half]], axis=0)
    first_a = []
    for d in (1, 2, 3, 0):
        to = (x + d) % 4
        rows = pl.ds(to * 256, 256)
        block = dot_nt(dense_re[rows, :], z1) + dot_nt(dense_im[rows, :], z2)
        block_a = block[:, :half].reshape(4, 64, half)
        block_b = block[:, half:].reshape(4, 64, half)
        for j in range(4):
            ysb[j, to] = block_b[j].astype(ysb.dtype)
            yown_b[j, to] = block_b[j]
        if d:
            ysa[d - 1] = block_a.astype(ysa.dtype)
            first_a.append(remote(ysa.at[d - 1], yra.at[d - 1], sya.at[d - 1], rya.at[d - 1], r, to * 4 + y))
            first_a[-1].start()
        else:
            yown_a[...] = block_a
    first_b = []
    for d in range(1, 4):
        to = (y + d) % 4
        first_b.append(remote(ysb.at[to], yrb.at[d - 1], syb.at[d - 1], ryb.at[d - 1], r, x * 4 + to))
        first_b[-1].start()
    sum_a = yown_a[...]
    for d in range(1, 4):
        first_a[d - 1].wait_recv()
        sum_a = sum_a + yra[d - 1].astype(jnp.float32)
    yown_a[...] = sum_a
    ys2[0] = sum_a.astype(ys2.dtype)
    second_a = []
    for d in range(1, 4):
        to = (y + d) % 4
        second_a.append(remote(ys2.at[0, to], yr2a.at[d - 1], sy2a.at[d - 1], ry2a.at[d - 1], r, x * 4 + to))
        second_a[-1].start()
    sum_b = yown_b[y]
    for d in range(1, 4):
        first_b[d - 1].wait_recv()
        sum_b = sum_b + yrb[d - 1].astype(jnp.float32)
    yown_b[0] = sum_b
    ys2[1] = sum_b.astype(ys2.dtype)
    second_b = []
    for d in range(1, 4):
        to = (x + d) % 4
        second_b.append(remote(ys2.at[1, to], yr2b.at[d - 1], sy2b.at[d - 1], ry2b.at[d - 1], r, to * 4 + y))
        second_b[-1].start()
    final_a = yown_a[y]
    for d in range(1, 4):
        second_a[d - 1].wait_recv()
        final_a = final_a + yr2a[d - 1].astype(jnp.float32)
    final_b = yown_b[0, x]
    for d in range(1, 4):
        second_b[d - 1].wait_recv()
        final_b = final_b + yr2b[d - 1].astype(jnp.float32)
    image_ref[:, :half] = final_a
    image_ref[:, half:] = final_b

    both = jnp.concatenate([final_a, final_b], axis=0)
    turned = jnp.concatenate([final_b, -final_a], axis=0)
    gram_re = dot_tn(both, both, HI)
    gram_im = dot_tn(both, turned, HI)
    rows = lax.broadcasted_iota(jnp.int32, (RANK, RANK), 0)
    cols = lax.broadcasted_iota(jnp.int32, (RANK, RANK), 1)
    hpart[...] = jnp.where(rows >= cols, gram_re, gram_im).reshape(16, 16, RANK)
    g1 = []
    for d in range(1, 16):
        to = (c + d) % 16
        g1.append(remote(hpart.at[to], hrecv.at[d - 1], sh1.at[d - 1], rh1.at[d - 1], r, to))
        g1[-1].start()
    acc = hpart[c]
    for d in range(1, 16):
        g1[d - 1].wait_recv()
        acc = acc + hrecv[d - 1]
    hrow[r] = acc
    g2 = []
    for d in range(1, 8):
        g2.append(remote(hrow.at[r], hrow.at[r], sh2.at[d - 1], rh2.at[d - 1], (r + d) % 8, c))
        g2[-1].start()
    for d in range(1, 8):
        g2[d - 1].wait_recv()
    acc = hrow[0]
    for i in range(1, 8):
        acc = acc + hrow[i]
    gram_ref[c] = acc
    g3 = []
    for d in range(1, 16):
        g3.append(remote(gram_ref.at[c], gram_ref.at[c], sh3.at[d - 1], rh3.at[d - 1], r, (c + d) % 16))
        g3[-1].start()
    for d in range(1, 16):
        g3[d - 1].wait_recv()
    for copy in [pair] + sends + spread + relay + first_a + first_b + second_a + second_b + g1 + g2 + g3:
        copy.wait_send()


def tail(dense_re, dense_im, qt):
    bf, f32 = jnp.bfloat16, jnp.float32
    dma = pltpu.SemaphoreType.DMA
    vm = pltpu.VMEM
    scratch = [
        vm((512, 512), f32), vm((256, 512), bf), vm((256, 512), bf), vm((4, 64, 512), bf), vm((3, 64, 512), bf), vm((512, 512), bf),
        vm((4, 64, 256), f32), vm((4, 4, 64, 256), f32), vm((3, 4, 64, 256), bf), vm((4, 4, 64, 256), bf),
        vm((3, 4, 64, 256), bf), vm((3, 4, 64, 256), bf), vm((2, 4, 64, 256), f32), vm((3, 64, 256), f32), vm((3, 64, 256), f32),
        vm((16, 16, RANK), f32), vm((15, 16, RANK), f32), vm((8, 16, RANK), f32),
        dma, dma, dma((3,)), dma((3,)), dma((3,)), dma((3,)), dma((4,)), dma((4,)), dma((3,)), dma((3,)), dma((3,)), dma((3,)),
        dma((3,)), dma((3,)), dma((3,)), dma((3,)), dma((15,)), dma((15,)), dma((7,)), dma((7,)), dma((15,)), dma((15,)),
    ]
    vmem = pl.BlockSpec(memory_space=pltpu.VMEM)
    return pl.pallas_call(
        tail_kernel,
        out_shape=(jax.ShapeDtypeStruct((64, 2 * RANK), f32), jax.ShapeDtypeStruct((16, 16, RANK), f32)),
        in_specs=[vmem] * 3,
        out_specs=(vmem, vmem),
        scratch_shapes=scratch,
        compiler_params=pltpu.CompilerParams(collective_id=1, has_side_effects=True, vmem_limit_bytes=48 << 20),
    )(dense_re, dense_im, qt)


def factor_inverse(diag):
    lane = lax.broadcasted_iota(jnp.int32, (NB, 4 * NB), 1)
    sub = lax.broadcasted_iota(jnp.int32, (NB, 4 * NB), 0)
    unit = (lane - 2 * NB == sub).astype(jnp.float32)
    unit_i = (lane - 3 * NB == sub).astype(jnp.float32)
    re, im = diag[:, :NB], diag[:, NB:]
    z = jnp.zeros((NB, 2 * NB), jnp.float32)
    w = jnp.concatenate([re, im, z], axis=1) + unit
    v = jnp.concatenate([-im, re, z], axis=1) + unit_i
    sub1 = sub[:, :1]
    for j in range(NB - 1):
        piv = w[j : j + 1, j : j + 1]
        below = sub1 > j
        c_re = jnp.where(below, w[:, j : j + 1], 0.0)
        c_im = jnp.where(below, w[:, NB + j : NB + j + 1], 0.0)
        inv = 1.0 / piv
        row = w[j : j + 1, :] * inv
        rov = v[j : j + 1, :] * inv
        w = w - (c_re * row + c_im * rov)
        v = v - (c_re * rov - c_im * row)
    d = jnp.sum(jnp.where(lane == sub, w, 0.0), axis=1, keepdims=True)
    return w[:, 2 * NB :] * lax.rsqrt(d)


def swapped(m):
    return jnp.concatenate([-m[:, NB:], m[:, :NB]], axis=1)


def chol_kernel(scale, g_ref, y_ref, out_ref, a_ref):
    n = RANK
    rows = y_ref.shape[0]
    panels = n // NB
    packed = g_ref[...]
    turned = packed.T
    sub = lax.broadcasted_iota(jnp.int32, (n, n), 0)
    lane = lax.broadcasted_iota(jnp.int32, (n, n), 1)
    g_re = jnp.where(sub >= lane, packed, turned)
    g_im = jnp.where(sub > lane, -turned, jnp.where(sub == lane, 0.0, packed))
    for k in range(panels):
        a_ref[:n, 2 * NB * k : 2 * NB * k + NB] = g_re[:, NB * k : NB * k + NB]
        a_ref[:n, 2 * NB * k + NB : 2 * NB * (k + 1)] = g_im[:, NB * k : NB * k + NB]
        a_ref[n:, 2 * NB * k : 2 * NB * k + NB] = y_ref[:, NB * k : NB * k + NB]
        a_ref[n:, 2 * NB * k + NB : 2 * NB * (k + 1)] = y_ref[:, n + NB * k : n + NB * k + NB]
    for k in range(panels):
        lo = k * NB
        inv = factor_inverse(a_ref[lo : lo + NB, 2 * lo : 2 * lo + 2 * NB])
        both = jnp.concatenate([inv, swapped(inv)], axis=0)
        ap = a_ref[lo + NB :, 2 * lo : 2 * lo + 2 * NB]
        low = dot_nt(ap, both, HI)
        solved = low[low.shape[0] - rows :] * scale
        out_ref[:, 0, lo : lo + NB] = solved[:, :NB]
        out_ref[:, 1, lo : lo + NB] = solved[:, NB:]
        left = panels - 1 - k
        if left:
            lk = low[: left * NB]
            q = jnp.concatenate([lk.reshape(left, NB, 2 * NB), swapped(lk).reshape(left, NB, 2 * NB)], axis=1)
            q = q.reshape(left * 2 * NB, 2 * NB)
            a_ref[lo + NB :, 2 * lo + 2 * NB :] -= dot_nt(low, q, HI)


def chol(g, y, scale):
    vmem = pl.BlockSpec(memory_space=pltpu.VMEM)
    return pl.pallas_call(
        functools.partial(chol_kernel, scale),
        out_shape=jax.ShapeDtypeStruct((y.shape[0], 2, RANK), jnp.float32),
        in_specs=[vmem] * 2,
        out_specs=vmem,
        scratch_shapes=[pltpu.VMEM((RANK + y.shape[0], 2 * RANK), jnp.float32)],
    )(g, y)


def body(reflection, focus_in, focus_out, ref_angle, element_order, q_start):
    dense_re, dense_im = head(reflection, element_order.reshape(1, -1), focus_in, focus_out, ref_angle)
    qt = jnp.transpose(q_start, (1, 2, 0)).reshape(2 * RANK, -1)
    image, gram = tail(dense_re, dense_im, qt)
    return chol(gram.reshape(RANK, RANK), image, math.sqrt(NF))


def solution(mesh):
    in_specs = (
        P(None, "col", "row"),
        P(None, "row", "col"),
        P(None, "row", None),
        P("row", "col"),
        P("row"),
        P("row", None, None),
    )
    out_specs = P(("row", "col"), None, None)
    return jax.shard_map(body, mesh=mesh, in_specs=in_specs, out_specs=out_specs, check_vma=False)
```

```python
import functools
import math

import jax
import jax.numpy as jnp
from jax import lax
from jax.experimental import pallas as pl
from jax.experimental.pallas import tpu as pltpu
from jax.sharding import PartitionSpec as P

NF = 8192
RANK = 256
PANEL_W = 512
NB = 32
HI = lax.Precision.HIGHEST
MESH = pl.DeviceIdType.MESH


def dot_nt(a, b, precision=None):
    return lax.dot_general(a, b, (((1,), (1,)), ((), ())), precision=precision, preferred_element_type=jnp.float32)


def dot_nn(a, b):
    return jnp.dot(a, b, preferred_element_type=jnp.float32)


def dot_tn(a, b, precision=None):
    return lax.dot_general(a, b, (((0,), (0,)), ((), ())), precision=precision, preferred_element_type=jnp.float32)


def remote(src, dst, send_sem, recv_sem, row, col):
    return pltpu.make_async_remote_copy(
        src_ref=src, dst_ref=dst, send_sem=send_sem, recv_sem=recv_sem, device_id=(row, col), device_id_type=MESH
    )


def cos_sin(angle):
    half = 0.5 * angle
    t = half * half
    s = -1.0 / 39916800.0
    for k in (1.0 / 362880.0, -1.0 / 5040.0, 1.0 / 120.0, -1.0 / 6.0, 1.0):
        s = s * t + k
    s = s * half
    c = 1.0 / 479001600.0
    for k in (-1.0 / 3628800.0, 1.0 / 40320.0, -1.0 / 720.0, 1.0 / 24.0, -0.5, 1.0):
        c = c * t + k
    return 1.0 - 2.0 * s * s, 2.0 * s * c


def front_kernel(
    refl_ref, order_ref, q_ref, focus_in_hbm, focus_out_hbm, angle_hbm, image_ref, gram_ref,
    gat, p_ref, f_ref, cosine, sine, cpart, crecv, zsend, zrecv, cfull, last_pair, last_recv, last_send, last_across, acc, dense_re, dense_im,
    qt, zown, zs1, zr1, zs2, zr2, zfull,
    yown_a, yown_b, ysa, ysb, yra, yrb, ys2, yr2a, yr2b,
    hpart, hrecv, hrow,
    local_sem, gs, gr, ps, pr, zs, zr, cs, cr, ws, wr,
    sz1, rz1, sz2, rz2, sz3, rz3, sz4, rz4, sya, rya, syb, ryb, sy2a, ry2a, sy2b, ry2b, sh1, rh1, sh2, rh2, sh3, rh3,
):
    r = lax.axis_index("row")
    c = lax.axis_index("col")
    z, core = r // 2, r % 2
    x, y = c // 4, c % 4
    other = 1 - core
    up = {"x": (x + 1) % 4, "y": (y + 1) % 4}
    down = {"x": (x + 3) % 4, "y": (y + 3) % 4}
    far_x, far_y = (x + 2) % 4, (y + 2) % 4
    left, right, low, high = down["x"], up["x"], down["y"], up["y"]

    loads = [
        pltpu.make_async_copy(focus_in_hbm, p_ref, local_sem.at[0]),
        pltpu.make_async_copy(focus_out_hbm, f_ref, local_sem.at[1]),
        pltpu.make_async_copy(angle_hbm, cosine, local_sem.at[2]),
    ]
    for copy in loads:
        copy.start()
    barrier = pltpu.get_barrier_semaphore()
    for d in range(1, 8):
        pl.semaphore_signal(barrier, inc=1, device_id=((r + d) % 8, c), device_id_type=MESH)
    for d in range(1, 16):
        pl.semaphore_signal(barrier, inc=1, device_id=(r, (c + d) % 16), device_id_type=MESH)

    sub = lax.broadcasted_iota(jnp.int32, (PANEL_W, PANEL_W), 0)
    for b in range(refl_ref.shape[2] // PANEL_W):
        lanes = pl.ds(b * PANEL_W, PANEL_W)
        place = order_ref[:, lanes] & (PANEL_W - 1)
        onehot = jnp.where(place == sub, 1.0, 0.0).astype(jnp.bfloat16)
        raw = jnp.concatenate([refl_ref[0, :32, lanes], refl_ref[1, :32, lanes], refl_ref[0, 32:, lanes], refl_ref[1, 32:, lanes]], axis=0)
        moved = dot_nt(raw, onehot).astype(jnp.bfloat16)
        gat[x, y, 0, :, lanes] = moved[:64]
        gat[x, y, 1, :, lanes] = moved[64:]
    pl.semaphore_wait(barrier, 22)

    copies = {}

    def send(name, sx, sy, h, piece=None):
        axis, way = name[-2], name[-1]
        to = (up if way == "+" else down)[axis]
        col = to * 4 + y if axis == "x" else x * 4 + to
        ref = gat.at[sx, sy, h] if piece is None else gat.at[sx, sy, h, pl.ds(32 * piece, 32)]
        i = len(copies)
        copies[name] = remote(ref, ref, gs.at[i], gr.at[i], r, col)
        copies[name].start()

    def got(*names):
        for name in names:
            copies[name + "+"].wait_recv()
            copies[name + "-"].wait_recv()

    def both(name, sx, sy, h):
        send(name + "+", sx, sy, h)
        send(name + "-", sx, sy, h)

    def gemm(s, parts):
        @pl.loop(0, 2)
        def _(n):
            lanes = pl.ds(pl.multiple_of(n * 256, 256), 256)
            rows = jnp.concatenate([gat[sx, sy, h] for sx, sy, h in parts], axis=0)
            by_re = dot_nn(rows, p_ref[0, :, lanes]).reshape(4, 2, 32, 256)
            by_im = dot_nn(rows, p_ref[1, :, lanes]).reshape(4, 2, 32, 256)
            cpart[s, 0, :, :, lanes] = by_re[:, 0] - by_im[:, 1]
            cpart[s, 1, :, :, lanes] = by_im[:, 0] + by_re[:, 1]

    pair, across, back, relay = {}, {}, {}, {}

    def start_pair(s):
        if s == 7:
            last_pair[...] = cpart[s, other].astype(jnp.bfloat16)
            pair[s] = remote(last_pair, last_recv, ps.at[s], pr.at[s], z * 2 + other, c)
        else:
            pair[s] = remote(cpart.at[s, other], crecv.at[s], ps.at[s], pr.at[s], z * 2 + other, c)
        pair[s].start()

    def start_across(s):
        pair[s].wait_recv()
        across[s] = []
        if s == 7:
            mine = cpart[s, core] + last_recv[...].astype(jnp.float32)
            last_send[...] = mine.astype(jnp.bfloat16)
        else:
            mine = cpart[s, core] + crecv[s]
        zsend[s] = mine
        for d in range(1, 4):
            to = (z + d) % 4
            if s == 7:
                src, dst = last_send.at[to], last_across.at[d - 1]
            else:
                src, dst = zsend.at[s, to], zrecv.at[s, d - 1]
            across[s].append(remote(src, dst, zs.at[s, d - 1], zr.at[s, d - 1], to * 2 + core, c))
            across[s][-1].start()

    def place_of(parts, q):
        first = jnp.int32(0)
        for i, (sx, sy, h) in enumerate(parts):
            first = first + jnp.where(q == i, 1, 0) * (sx * 256 + sy * 64 + h * 32)
        return pl.multiple_of(first, 32)

    def start_back(s, parts):
        total = zsend[s, z]
        for d in range(1, 4):
            across[s][d - 1].wait_recv()
            total = total + (last_across[d - 1].astype(jnp.float32) if s == 7 else zrecv[s, d - 1])
        mine = pl.ds(place_of(parts, z), 32)
        cfull[core, mine, :] = total.astype(jnp.bfloat16)
        ref = cfull.at[core, mine, :]
        back[s] = []
        for d in range(1, 4):
            back[s].append(remote(ref, ref, cs.at[s, d - 1], cr.at[s, d - 1], (z + d) % 4 * 2 + core, c))
            back[s][-1].start()
        relay[s] = [remote(ref, ref, ws.at[s, 0], wr.at[s, 0], z * 2 + other, c)]
        relay[s][0].start()

    def start_relay(s, parts):
        for d in range(1, 4):
            back[s][d - 1].wait_recv()
            ref = cfull.at[core, pl.ds(place_of(parts, (z + 4 - d) % 4), 32), :]
            relay[s].append(remote(ref, ref, ws.at[s, d], wr.at[s, d], z * 2 + other, c))
            relay[s][-1].start()

    def finish(s):
        for copy in relay[s]:
            copy.wait_recv()

    batches = [
        [(x, y, 0), (x, y, 1), (left, y, 0), (right, y, 0)],
        [(x, low, 1), (x, high, 1), (x, low, 0), (x, high, 0)],
        [(left, y, 1), (right, y, 1), (x, far_y, 1), (far_x, y, 0)],
        [(left, low, 0), (left, high, 0), (left, low, 1), (right, low, 1)],
        [(right, low, 0), (right, high, 0), (left, high, 1), (right, high, 1)],
        [(x, far_y, 0), (far_x, y, 1), (far_x, low, 0), (far_x, high, 0)],
        [(left, far_y, 1), (right, far_y, 1), (left, far_y, 0), (far_x, low, 1)],
        [(right, far_y, 0), (far_x, high, 1), (far_x, far_y, 0), (far_x, far_y, 1)],
    ]

    def progress(s):
        if 0 <= s - 1 < 8:
            start_across(s - 1)
        if 0 <= s - 2 < 8:
            start_back(s - 2, batches[s - 2])
        if 0 <= s - 3 < 8:
            start_relay(s - 3, batches[s - 3])
        if 0 <= s - 4 < 8:
            finish(s - 4)

    both("Ax", x, y, 0)
    both("By", x, y, 1)
    both("Ay", x, y, 0)
    both("Bx", x, y, 1)
    loads[0].wait()
    for s in range(8):
        if s == 0:
            got("Ax")
            send("Aqx+", left, y, 0, 0)
            send("Aqx-", right, y, 0, 1)
            got("By")
            send("Bqy+", x, low, 1, 0)
            send("Bqy-", x, high, 1, 1)
            both("A1y", left, y, 0)
            both("B1x", x, low, 1)
            both("A2y", right, y, 0)
            both("B2x", x, high, 1)
        elif s == 1:
            got("Ay")
            send("Aq0y+", x, low, 0, 0)
            send("Aq0y-", x, high, 0, 1)
            got("Bx")
            send("Bq0x+", left, y, 1, 0)
            send("Bq0x-", right, y, 1, 1)
        elif s == 2:
            got("Aqx")
            both("A3y", far_x, y, 0)
            got("Bqy")
            both("B3x", x, far_y, 1)
        elif s == 3:
            got("A1y")
            send("Aq1y+", left, low, 0, 0)
            send("Aq1y-", left, high, 0, 1)
            got("B1x")
            send("Bq1x+", left, low, 1, 0)
            send("Bq1x-", right, low, 1, 1)
        elif s == 4:
            got("A2y")
            send("Aq2y+", right, low, 0, 0)
            send("Aq2y-", right, high, 0, 1)
            got("B2x")
            send("Bq2x+", left, high, 1, 0)
            send("Bq2x-", right, high, 1, 1)
        elif s == 5:
            got("Aq0y", "Bq0x", "A3y")
            send("Aq3y+", far_x, low, 0, 0)
            send("Aq3y-", far_x, high, 0, 1)
            got("B3x")
            send("Bq3x+", left, far_y, 1, 0)
            send("Bq3x-", right, far_y, 1, 1)
        elif s == 6:
            got("Aq1y", "Bq1x")
        else:
            got("Aq2y", "Bq2x", "Aq3y", "Bq3x")
        progress(s)
        gemm(s, batches[s])
        start_pair(s)
        if s == 2:
            loads[2].wait()

            @pl.loop(0, 8)
            def _(m):
                rows = pl.ds(pl.multiple_of(m * 128, 128), 128)
                cosine[rows, :], sine[rows, :] = cos_sin(cosine[rows, :])
        if s == 3:
            qt[0] = q_ref[:, 0, :].T
            qt[1] = q_ref[:, 1, :].T

    def outer(to, rows):
        lanes = pl.ds(pl.multiple_of(to * 256, 256), 256)
        f_re, f_im = f_ref[0, rows, lanes], f_ref[1, rows, lanes]
        c_re, c_im = cfull[0, lanes, :], cfull[1, lanes, :]
        return dot_nn(f_re, c_re) - dot_nn(f_im, c_im), dot_nn(f_re, c_im) + dot_nn(f_im, c_re)

    progress(8)
    finish(5)
    loads[1].wait()

    @pl.loop(0, 8)
    def _(m):
        rows = pl.ds(pl.multiple_of(m * 128, 128), 128)
        acc[0, rows, :], acc[1, rows, :] = outer(x, rows)

    start_back(7, batches[7])
    start_relay(6, batches[6])
    finish(6)

    @pl.loop(0, 8)
    def _(m):
        rows = pl.ds(pl.multiple_of(m * 128, 128), 128)
        add_re, add_im = outer(left, rows)
        acc[0, rows, :] += add_re
        acc[1, rows, :] += add_im

    start_relay(7, batches[7])
    finish(7)

    @pl.loop(0, 8)
    def _(m):
        rows = pl.ds(pl.multiple_of(m * 128, 128), 128)
        right_re, right_im = outer(right, rows)
        far_re, far_im = outer(far_x, rows)
        outer_re = acc[0, rows, :] + (right_re + far_re)
        outer_im = acc[1, rows, :] + (right_im + far_im)
        co, si = cosine[rows, :], sine[rows, :]
        dense_re[rows, :] = (outer_re * co + outer_im * si).astype(jnp.bfloat16)
        dense_im[rows, :] = (outer_im * co - outer_re * si).astype(jnp.bfloat16)


    half = RANK

    def z_half(h, sign):
        return dot_nn(qt[h], dense_re[...]) + sign * dot_nn(qt[1 - h], dense_im[...])

    sign = (1 - 2 * core).astype(jnp.float32)
    zs1[...] = z_half(other, -sign).astype(jnp.bfloat16)
    swap = remote(zs1, zr1, sz1, rz1, z * 2 + other, c)
    swap.start()
    zown[...] = z_half(core, sign)
    swap.wait_recv()
    mine = zown[...] + zr1[...].astype(jnp.float32)
    quarter = half // 4
    zs2[...] = mine.reshape(4, quarter, -1).astype(zs2.dtype)
    zown[...] = mine
    sends = []
    for d in range(1, 4):
        to = (z + d) % 4
        sends.append(remote(zs2.at[to], zr2.at[d - 1], sz2.at[d - 1], rz2.at[d - 1], to * 2 + core, c))
        sends[-1].start()
    total = zown[pl.ds(z * quarter, quarter), :]
    for d in range(1, 4):
        sends[d - 1].wait_recv()
        total = total + zr2[d - 1].astype(jnp.float32)
    slot = core * half + z * quarter
    own = zfull.at[pl.ds(slot, quarter), :]
    zfull[pl.ds(slot, quarter), :] = total.astype(jnp.bfloat16)
    spread = []
    for d in range(1, 4):
        to = (z + d) % 4
        spread.append(remote(own, own, sz3.at[d - 1], rz3.at[d - 1], to * 2 + core, c))
        spread[-1].start()
    hand = [remote(own, own, sz4.at[0], rz4.at[0], z * 2 + other, c)]
    hand[0].start()
    for d in range(1, 4):
        spread[d - 1].wait_recv()
        origin = (z + 4 - d) % 4
        part = zfull.at[pl.ds(core * half + origin * quarter, quarter), :]
        hand.append(remote(part, part, sz4.at[d], rz4.at[d], z * 2 + other, c))
        hand[-1].start()
    for d in range(4):
        hand[d].wait_recv()

    z1 = zfull[...]
    z2 = jnp.concatenate([-z1[half:], z1[:half]], axis=0)
    first_a = []
    for d in (1, 2, 3, 0):
        to = (x + d) % 4
        rows = pl.ds(to * 256, 256)
        block = dot_nt(dense_re[rows, :], z1) + dot_nt(dense_im[rows, :], z2)
        block_a = block[:, :half].reshape(4, 64, half)
        block_b = block[:, half:].reshape(4, 64, half)
        for j in range(4):
            ysb[j, to] = block_b[j].astype(ysb.dtype)
            yown_b[j, to] = block_b[j]
        if d:
            ysa[d - 1] = block_a.astype(ysa.dtype)
            first_a.append(remote(ysa.at[d - 1], yra.at[d - 1], sya.at[d - 1], rya.at[d - 1], r, to * 4 + y))
            first_a[-1].start()
        else:
            yown_a[...] = block_a
    first_b = []
    for d in range(1, 4):
        to = (y + d) % 4
        first_b.append(remote(ysb.at[to], yrb.at[d - 1], syb.at[d - 1], ryb.at[d - 1], r, x * 4 + to))
        first_b[-1].start()
    sum_a = yown_a[...]
    for d in range(1, 4):
        first_a[d - 1].wait_recv()
        sum_a = sum_a + yra[d - 1].astype(jnp.float32)
    yown_a[...] = sum_a
    ys2[0] = sum_a.astype(ys2.dtype)
    second_a = []
    for d in range(1, 4):
        to = (y + d) % 4
        second_a.append(remote(ys2.at[0, to], yr2a.at[d - 1], sy2a.at[d - 1], ry2a.at[d - 1], r, x * 4 + to))
        second_a[-1].start()
    sum_b = yown_b[y]
    for d in range(1, 4):
        first_b[d - 1].wait_recv()
        sum_b = sum_b + yrb[d - 1].astype(jnp.float32)
    yown_b[0] = sum_b
    ys2[1] = sum_b.astype(ys2.dtype)
    second_b = []
    for d in range(1, 4):
        to = (x + d) % 4
        second_b.append(remote(ys2.at[1, to], yr2b.at[d - 1], sy2b.at[d - 1], ry2b.at[d - 1], r, to * 4 + y))
        second_b[-1].start()
    final_a = yown_a[y]
    for d in range(1, 4):
        second_a[d - 1].wait_recv()
        final_a = final_a + yr2a[d - 1].astype(jnp.float32)
    final_b = yown_b[0, x]
    for d in range(1, 4):
        second_b[d - 1].wait_recv()
        final_b = final_b + yr2b[d - 1].astype(jnp.float32)
    image_ref[:, :half] = final_a
    image_ref[:, half:] = final_b

    both = jnp.concatenate([final_a, final_b], axis=0)
    turned = jnp.concatenate([final_b, -final_a], axis=0)
    gram_re = dot_tn(both, both, HI)
    gram_im = dot_tn(both, turned, HI)
    rows = lax.broadcasted_iota(jnp.int32, (RANK, RANK), 0)
    cols = lax.broadcasted_iota(jnp.int32, (RANK, RANK), 1)
    hpart[...] = jnp.where(rows >= cols, gram_re, gram_im).reshape(16, 16, RANK)
    g1 = []
    for d in range(1, 16):
        to = (c + d) % 16
        g1.append(remote(hpart.at[to], hrecv.at[d - 1], sh1.at[d - 1], rh1.at[d - 1], r, to))
        g1[-1].start()
    acc = hpart[c]
    for d in range(1, 16):
        g1[d - 1].wait_recv()
        acc = acc + hrecv[d - 1]
    hrow[r] = acc
    g2 = []
    for d in range(1, 8):
        g2.append(remote(hrow.at[r], hrow.at[r], sh2.at[d - 1], rh2.at[d - 1], (r + d) % 8, c))
        g2[-1].start()
    for d in range(1, 8):
        g2[d - 1].wait_recv()
    acc = hrow[0]
    for i in range(1, 8):
        acc = acc + hrow[i]
    gram_ref[c] = acc
    g3 = []
    for d in range(1, 16):
        g3.append(remote(gram_ref.at[c], gram_ref.at[c], sh3.at[d - 1], rh3.at[d - 1], r, (c + d) % 16))
        g3[-1].start()
    for d in range(1, 16):
        g3[d - 1].wait_recv()
    for copy in list(copies.values()) + [pair[s] for s in range(8)]:
        copy.wait_send()
    for s in range(8):
        for copy in across[s] + back[s] + relay[s]:
            copy.wait_send()
    for copy in [swap] + sends + spread + hand + first_a + first_b + second_a + second_b + g1 + g2 + g3:
        copy.wait_send()


def front(reflection, order, q, focus_in, focus_out, ref_angle):
    bf, f32 = jnp.bfloat16, jnp.float32
    vm, dma = pltpu.VMEM, pltpu.SemaphoreType.DMA
    vmem = pl.BlockSpec(memory_space=pltpu.VMEM)
    anywhere = pl.BlockSpec(memory_space=pl.ANY)
    scratch = [
        vm((4, 4, 2, 64, 2048), bf), vm((2, 2048, 512), bf), vm((2, 1024, 1024), bf), vm((1024, 512), f32), vm((1024, 512), f32),
        vm((8, 2, 4, 32, 512), f32), vm((8, 4, 32, 512), f32), vm((8, 4, 32, 512), f32), vm((8, 3, 32, 512), f32), vm((2, 1024, 512), bf),
        vm((4, 32, 512), bf), vm((4, 32, 512), bf), vm((4, 32, 512), bf), vm((3, 32, 512), bf),
        vm((2, 1024, 512), f32), vm((1024, 512), bf), vm((1024, 512), bf),
        vm((2, RANK, 1024), bf), vm((256, 512), f32), vm((256, 512), bf), vm((256, 512), bf), vm((4, 64, 512), bf), vm((3, 64, 512), bf), vm((512, 512), bf),
        vm((4, 64, 256), f32), vm((4, 4, 64, 256), f32), vm((3, 4, 64, 256), bf), vm((4, 4, 64, 256), bf),
        vm((3, 4, 64, 256), bf), vm((3, 4, 64, 256), bf), vm((2, 4, 64, 256), bf), vm((3, 64, 256), bf), vm((3, 64, 256), bf),
        vm((16, 16, RANK), f32), vm((15, 16, RANK), f32), vm((8, 16, RANK), f32),
        dma((3,)), dma((40,)), dma((40,)), dma((8,)), dma((8,)), dma((8, 3)), dma((8, 3)), dma((8, 3)), dma((8, 3)), dma((8, 4)), dma((8, 4)),
        dma, dma, dma((3,)), dma((3,)), dma((3,)), dma((3,)), dma((4,)), dma((4,)), dma((3,)), dma((3,)), dma((3,)), dma((3,)),
        dma((3,)), dma((3,)), dma((3,)), dma((3,)), dma((15,)), dma((15,)), dma((7,)), dma((7,)), dma((15,)), dma((15,)),
    ]
    return pl.pallas_call(
        front_kernel,
        out_shape=(jax.ShapeDtypeStruct((64, 2 * RANK), f32), jax.ShapeDtypeStruct((16, 16, RANK), f32)),
        in_specs=[vmem, vmem, vmem, anywhere, anywhere, anywhere],
        out_specs=(vmem, vmem),
        scratch_shapes=scratch,
        compiler_params=pltpu.CompilerParams(collective_id=0, has_side_effects=True, vmem_limit_bytes=62 << 20),
    )(reflection, order, q, focus_in, focus_out, ref_angle)


def bc(w, j):
    return jnp.broadcast_to(w[:, j:j+1], w.shape)

def rowb(w, j):
    return jnp.broadcast_to(w[j:j+1, :], w.shape)

def factor_inverse(diag):
    lane = lax.broadcasted_iota(jnp.int32, (NB, 4 * NB), 1)
    sub = lax.broadcasted_iota(jnp.int32, (NB, 4 * NB), 0)
    unit = (lane - 2 * NB == sub).astype(jnp.float32)
    unit_i = (lane - 3 * NB == sub).astype(jnp.float32)
    re, im = diag[:, :NB], diag[:, NB:]
    z = jnp.zeros((NB, 2 * NB), jnp.float32)
    w = jnp.concatenate([re, im, z], axis=1) + unit
    v = jnp.concatenate([-im, re, z], axis=1) + unit_i
    for base in range(0, NB, 8):
        cols = [(bc(w, j), bc(w, NB + j)) for j in range(base, base + 8)]
        while cols:
            (a_re, a_im), (b_re, b_im) = cols[:2]
            cols = cols[2:]
            j = base + 8 - len(cols) - 2
            p, q = a_re[j : j + 1], b_re[j + 1 : j + 2]
            s_re, s_im = a_re[j + 1 : j + 2], a_im[j + 1 : j + 2]
            det = 1.0 / (p * q - (s_re * s_re + s_im * s_im))
            pd, qd, sd_re, sd_im = p * det, q * det, s_re * det, s_im * det
            after = []
            for c_re, c_im in cols:
                x_re, x_im, y_re, y_im = c_re[j : j + 1], c_im[j : j + 1], c_re[j + 1 : j + 2], c_im[j + 1 : j + 2]
                g_re = qd * x_re - (sd_re * y_re + sd_im * y_im)
                g_im = qd * x_im - (sd_re * y_im - sd_im * y_re)
                h_re = pd * y_re - (sd_re * x_re - sd_im * x_im)
                h_im = pd * y_im - (sd_re * x_im + sd_im * x_re)
                after.append((
                    c_re - ((a_re * g_re - a_im * g_im) + (b_re * h_re - b_im * h_im)),
                    c_im - ((a_re * g_im + a_im * g_re) + (b_re * h_im + b_im * h_re)),
                ))
            cols = after
            top = 1.0 / p
            w0, v0, w1, v1 = w[j : j + 1, :], v[j : j + 1, :], w[j + 1 : j + 2, :], v[j + 1 : j + 2, :]
            u0 = qd * w0 - (sd_re * w1 - sd_im * v1)
            t0 = qd * v0 - (sd_re * v1 + sd_im * w1)
            u1 = pd * w1 - (sd_re * w0 + sd_im * v0)
            t1 = pd * v1 - (sd_re * v0 - sd_im * w0)
            second = sub == j + 1
            below = sub > j + 1
            x0, y0 = (s_re * w0 + s_im * v0) * top, (s_re * v0 - s_im * w0) * top
            dw = (a_re * u0 + a_im * t0) + (b_re * u1 + b_im * t1)
            dv = (a_re * t0 - a_im * u0) + (b_re * t1 - b_im * u1)
            w = w - jnp.where(below, dw, jnp.where(second, x0, 0.0))
            v = v - jnp.where(below, dv, jnp.where(second, y0, 0.0))

    d = jnp.sum(jnp.where(lane == sub, w, 0.0), axis=1, keepdims=True)
    return w[:, 2 * NB :] * lax.rsqrt(d)


def swapped(m):
    return jnp.concatenate([-m[:, NB:], m[:, :NB]], axis=1)


def chol_kernel(scale, g_ref, y_ref, out_ref, a_ref):
    n = RANK
    rows = y_ref.shape[0]
    panels = n // NB
    packed = g_ref[...]
    turned = packed.T
    sub = lax.broadcasted_iota(jnp.int32, (n, n), 0)
    lane = lax.broadcasted_iota(jnp.int32, (n, n), 1)
    g_re = jnp.where(sub >= lane, packed, turned)
    g_im = jnp.where(sub > lane, -turned, jnp.where(sub == lane, 0.0, packed))
    for k in range(panels):
        a_ref[:n, 2 * NB * k : 2 * NB * k + NB] = g_re[:, NB * k : NB * k + NB]
        a_ref[:n, 2 * NB * k + NB : 2 * NB * (k + 1)] = g_im[:, NB * k : NB * k + NB]
        a_ref[n:, 2 * NB * k : 2 * NB * k + NB] = y_ref[:, NB * k : NB * k + NB]
        a_ref[n:, 2 * NB * k + NB : 2 * NB * (k + 1)] = y_ref[:, n + NB * k : n + NB * k + NB]
    diag = a_ref[:NB, : 2 * NB]
    for k in range(panels):
        lo = k * NB
        inv = factor_inverse(diag)
        both = jnp.concatenate([inv, swapped(inv)], axis=0)
        left = panels - 1 - k
        if left:
            nxt = dot_nt(a_ref[lo + NB : lo + 2 * NB, 2 * lo : 2 * lo + 2 * NB], both, HI)
            turn = jnp.concatenate([nxt, swapped(nxt)], axis=0)
            diag = a_ref[lo + NB : lo + 2 * NB, 2 * lo + 2 * NB : 2 * lo + 4 * NB] - dot_nt(nxt, turn, HI)
        low = dot_nt(a_ref[lo + NB :, 2 * lo : 2 * lo + 2 * NB], both, HI)
        solved = low[low.shape[0] - rows :] * scale
        out_ref[:, 0, lo : lo + NB] = solved[:, :NB]
        out_ref[:, 1, lo : lo + NB] = solved[:, NB:]
        if left:
            lk = low[: left * NB]
            q = jnp.concatenate([lk.reshape(left, NB, 2 * NB), swapped(lk).reshape(left, NB, 2 * NB)], axis=1)
            q = q.reshape(left * 2 * NB, 2 * NB)
            a_ref[lo + NB :, 2 * lo + 2 * NB :] -= dot_nt(low, q, HI)


def chol(g, y, scale):
    vmem = pl.BlockSpec(memory_space=pltpu.VMEM)
    return pl.pallas_call(
        functools.partial(chol_kernel, scale),
        out_shape=jax.ShapeDtypeStruct((y.shape[0], 2, RANK), jnp.float32),
        in_specs=[vmem] * 2,
        out_specs=vmem,
        scratch_shapes=[pltpu.VMEM((RANK + y.shape[0], 2 * RANK), jnp.float32)],
    )(g, y)


def body(reflection, focus_in, focus_out, ref_angle, element_order, q_start):
    image, gram = front(reflection, element_order.reshape(1, -1), q_start, focus_in, focus_out, ref_angle)
    return chol(gram.reshape(RANK, RANK), image, math.sqrt(NF))


def solution(mesh):
    in_specs = (
        P(None, "col", "row"),
        P(None, "row", "col"),
        P(None, "row", None),
        P("row", "col"),
        P("row"),
        P("row", None, None),
    )
    out_specs = P(("row", "col"), None, None)
    return jax.shard_map(body, mesh=mesh, in_specs=in_specs, out_specs=out_specs, check_vma=False)
```

```python
import functools
import math

import jax
import jax.numpy as jnp
from jax import lax
from jax.experimental import pallas as pl
from jax.experimental.pallas import tpu as pltpu
from jax.sharding import PartitionSpec as P

NF = 8192
RANK = 256
PANEL_W = 512
NB = 64
HI = lax.Precision.HIGHEST
MESH = pl.DeviceIdType.MESH


def dot_nt(a, b, precision=None):
    return lax.dot_general(a, b, (((1,), (1,)), ((), ())), precision=precision, preferred_element_type=jnp.float32)


def dot_nn(a, b):
    return jnp.dot(a, b, preferred_element_type=jnp.float32)


def dot_tn(a, b, precision=None):
    return lax.dot_general(a, b, (((0,), (0,)), ((), ())), precision=precision, preferred_element_type=jnp.float32)


def remote(src, dst, send_sem, recv_sem, row, col):
    return pltpu.make_async_remote_copy(
        src_ref=src, dst_ref=dst, send_sem=send_sem, recv_sem=recv_sem, device_id=(row, col), device_id_type=MESH
    )


def cos_sin(angle):
    half = 0.5 * angle
    t = half * half
    s = -1.0 / 39916800.0
    for k in (1.0 / 362880.0, -1.0 / 5040.0, 1.0 / 120.0, -1.0 / 6.0, 1.0):
        s = s * t + k
    s = s * half
    c = 1.0 / 479001600.0
    for k in (-1.0 / 3628800.0, 1.0 / 40320.0, -1.0 / 720.0, 1.0 / 24.0, -0.5, 1.0):
        c = c * t + k
    return 1.0 - 2.0 * s * s, 2.0 * s * c


def front_kernel(
    refl_ref, order_ref, q_ref, focus_in_hbm, focus_out_hbm, angle_hbm, image_ref, gram_ref,
    gat, p_ref, f_ref, cosine, sine, cpart, crecv, zsend, zrecv, cfull, last_pair, last_recv, last_send, last_across, acc, dense_re, dense_im,
    qt, zown, zs1, zr1, zs2, zr2, zfull,
    yown_a, yown_b, ysa, ysb, yra, yrb, ys2, yr2a, yr2b,
    hpart, hrecv, hrow,
    local_sem, gs, gr, ps, pr, zs, zr, cs, cr, ws, wr,
    sz1, rz1, sz2, rz2, sz3, rz3, sz4, rz4, sya, rya, syb, ryb, sy2a, ry2a, sy2b, ry2b, sh1, rh1, sh2, rh2, sh3, rh3,
):
    r = lax.axis_index("row")
    c = lax.axis_index("col")
    z, core = r // 2, r % 2
    x, y = c // 4, c % 4
    other = 1 - core
    up = {"x": (x + 1) % 4, "y": (y + 1) % 4}
    down = {"x": (x + 3) % 4, "y": (y + 3) % 4}
    far_x, far_y = (x + 2) % 4, (y + 2) % 4
    left, right, low, high = down["x"], up["x"], down["y"], up["y"]

    loads = [
        pltpu.make_async_copy(focus_in_hbm, p_ref, local_sem.at[0]),
        pltpu.make_async_copy(focus_out_hbm, f_ref, local_sem.at[1]),
        pltpu.make_async_copy(angle_hbm, cosine, local_sem.at[2]),
    ]
    for copy in loads:
        copy.start()
    barrier = pltpu.get_barrier_semaphore()
    for d in range(1, 8):
        pl.semaphore_signal(barrier, inc=1, device_id=((r + d) % 8, c), device_id_type=MESH)
    for d in range(1, 16):
        pl.semaphore_signal(barrier, inc=1, device_id=(r, (c + d) % 16), device_id_type=MESH)

    sub = lax.broadcasted_iota(jnp.int32, (PANEL_W, PANEL_W), 0)
    for b in range(refl_ref.shape[2] // PANEL_W):
        lanes = pl.ds(b * PANEL_W, PANEL_W)
        place = order_ref[:, lanes] & (PANEL_W - 1)
        onehot = jnp.where(place == sub, 1.0, 0.0).astype(jnp.bfloat16)
        raw = jnp.concatenate([refl_ref[0, :32, lanes], refl_ref[1, :32, lanes], refl_ref[0, 32:, lanes], refl_ref[1, 32:, lanes]], axis=0)
        moved = dot_nt(raw, onehot).astype(jnp.bfloat16)
        gat[x, y, 0, :, lanes] = moved[:64]
        gat[x, y, 1, :, lanes] = moved[64:]
    pl.semaphore_wait(barrier, 22)

    copies = {}

    def send(name, sx, sy, h, piece=None):
        axis, way = name[-2], name[-1]
        to = (up if way == "+" else down)[axis]
        col = to * 4 + y if axis == "x" else x * 4 + to
        ref = gat.at[sx, sy, h] if piece is None else gat.at[sx, sy, h, pl.ds(32 * piece, 32)]
        i = len(copies)
        copies[name] = remote(ref, ref, gs.at[i], gr.at[i], r, col)
        copies[name].start()

    def got(*names):
        for name in names:
            copies[name + "+"].wait_recv()
            copies[name + "-"].wait_recv()

    def both(name, sx, sy, h):
        send(name + "+", sx, sy, h)
        send(name + "-", sx, sy, h)

    def gemm(s, parts):
        @pl.loop(0, 2)
        def _(n):
            lanes = pl.ds(pl.multiple_of(n * 256, 256), 256)
            rows = jnp.concatenate([gat[sx, sy, h] for sx, sy, h in parts], axis=0)
            by_re = dot_nn(rows, p_ref[0, :, lanes]).reshape(4, 2, 32, 256)
            by_im = dot_nn(rows, p_ref[1, :, lanes]).reshape(4, 2, 32, 256)
            cpart[s, 0, :, :, lanes] = by_re[:, 0] - by_im[:, 1]
            cpart[s, 1, :, :, lanes] = by_im[:, 0] + by_re[:, 1]

    pair, across, back, relay = {}, {}, {}, {}

    def start_pair(s):
        if s == 7:
            last_pair[...] = cpart[s, other].astype(jnp.bfloat16)
            pair[s] = remote(last_pair, last_recv, ps.at[s], pr.at[s], z * 2 + other, c)
        else:
            pair[s] = remote(cpart.at[s, other], crecv.at[s], ps.at[s], pr.at[s], z * 2 + other, c)
        pair[s].start()

    def start_across(s):
        pair[s].wait_recv()
        across[s] = []
        if s == 7:
            mine = cpart[s, core] + last_recv[...].astype(jnp.float32)
            last_send[...] = mine.astype(jnp.bfloat16)
        else:
            mine = cpart[s, core] + crecv[s]
        zsend[s] = mine
        for d in range(1, 4):
            to = (z + d) % 4
            if s == 7:
                src, dst = last_send.at[to], last_across.at[d - 1]
            else:
                src, dst = zsend.at[s, to], zrecv.at[s, d - 1]
            across[s].append(remote(src, dst, zs.at[s, d - 1], zr.at[s, d - 1], to * 2 + core, c))
            across[s][-1].start()

    def place_of(parts, q):
        first = jnp.int32(0)
        for i, (sx, sy, h) in enumerate(parts):
            first = first + jnp.where(q == i, 1, 0) * (sx * 256 + sy * 64 + h * 32)
        return pl.multiple_of(first, 32)

    def start_back(s, parts):
        total = zsend[s, z]
        for d in range(1, 4):
            across[s][d - 1].wait_recv()
            total = total + (last_across[d - 1].astype(jnp.float32) if s == 7 else zrecv[s, d - 1])
        mine = pl.ds(place_of(parts, z), 32)
        cfull[core, mine, :] = total.astype(jnp.bfloat16)
        ref = cfull.at[core, mine, :]
        back[s] = []
        for d in range(1, 4):
            back[s].append(remote(ref, ref, cs.at[s, d - 1], cr.at[s, d - 1], (z + d) % 4 * 2 + core, c))
            back[s][-1].start()
        relay[s] = [remote(ref, ref, ws.at[s, 0], wr.at[s, 0], z * 2 + other, c)]
        relay[s][0].start()

    def start_relay(s, parts):
        for d in range(1, 4):
            back[s][d - 1].wait_recv()
            ref = cfull.at[core, pl.ds(place_of(parts, (z + 4 - d) % 4), 32), :]
            relay[s].append(remote(ref, ref, ws.at[s, d], wr.at[s, d], z * 2 + other, c))
            relay[s][-1].start()

    def finish(s):
        for copy in relay[s]:
            copy.wait_recv()

    batches = [
        [(x, y, 0), (x, y, 1), (left, y, 0), (right, y, 0)],
        [(x, low, 1), (x, high, 1), (x, low, 0), (x, high, 0)],
        [(left, y, 1), (right, y, 1), (x, far_y, 1), (far_x, y, 0)],
        [(left, low, 0), (left, high, 0), (left, low, 1), (right, low, 1)],
        [(right, low, 0), (right, high, 0), (left, high, 1), (right, high, 1)],
        [(x, far_y, 0), (far_x, y, 1), (far_x, low, 0), (far_x, high, 0)],
        [(left, far_y, 1), (right, far_y, 1), (left, far_y, 0), (right, far_y, 0)],
        [(far_x, low, 1), (far_x, high, 1), (far_x, far_y, 0), (far_x, far_y, 1)],
    ]

    def progress(s):
        if 0 <= s - 1 < 8:
            start_across(s - 1)
        if 0 <= s - 2 < 8:
            start_back(s - 2, batches[s - 2])
        if 0 <= s - 3 < 8:
            start_relay(s - 3, batches[s - 3])
        if 0 <= s - 4 < 8:
            finish(s - 4)

    both("Ax", x, y, 0)
    both("By", x, y, 1)
    both("Ay", x, y, 0)
    both("Bx", x, y, 1)
    loads[0].wait()
    for s in range(8):
        if s == 0:
            got("Ax")
            send("Aqx+", left, y, 0, 0)
            send("Aqx-", right, y, 0, 1)
            got("By")
            send("Bqy+", x, low, 1, 0)
            send("Bqy-", x, high, 1, 1)
            both("A1y", left, y, 0)
            both("B1x", x, low, 1)
            both("A2y", right, y, 0)
            both("B2x", x, high, 1)
        elif s == 1:
            got("Ay")
            send("Aq0y+", x, low, 0, 0)
            send("Aq0y-", x, high, 0, 1)
            got("Bx")
            send("Bq0x+", left, y, 1, 0)
            send("Bq0x-", right, y, 1, 1)
        elif s == 2:
            got("Aqx")
            both("A3y", far_x, y, 0)
            got("Bqy")
            both("B3x", x, far_y, 1)
        elif s == 3:
            got("A1y")
            send("Aq1y+", left, low, 0, 0)
            send("Aq1y-", left, high, 0, 1)
            got("B1x")
            send("Bq1x+", left, low, 1, 0)
            send("Bq1x-", right, low, 1, 1)
        elif s == 4:
            got("A2y")
            send("Aq2y+", right, low, 0, 0)
            send("Aq2y-", right, high, 0, 1)
            got("B2x")
            send("Bq2x+", left, high, 1, 0)
            send("Bq2x-", right, high, 1, 1)
        elif s == 5:
            got("Aq0y", "Bq0x", "A3y")
            send("Aq3y+", far_x, low, 0, 0)
            send("Aq3y-", far_x, high, 0, 1)
            got("B3x")
            send("Bq3x+", left, far_y, 1, 0)
            send("Bq3x-", right, far_y, 1, 1)
        elif s == 6:
            got("Aq1y", "Aq2y")
        else:
            got("Bq1x", "Bq2x", "Aq3y", "Bq3x")
        progress(s)
        gemm(s, batches[s])
        start_pair(s)
        if s == 2:
            loads[2].wait()

            @pl.loop(0, 8)
            def _(m):
                rows = pl.ds(pl.multiple_of(m * 128, 128), 128)
                cosine[rows, :], sine[rows, :] = cos_sin(cosine[rows, :])
        if s == 3:
            qt[0] = q_ref[:, 0, :].T
            qt[1] = q_ref[:, 1, :].T

    def outer(to, rows):
        lanes = pl.ds(pl.multiple_of(to * 256, 256), 256)
        f_re, f_im = f_ref[0, rows, lanes], f_ref[1, rows, lanes]
        c_re, c_im = cfull[0, lanes, :], cfull[1, lanes, :]
        return dot_nn(f_re, c_re) - dot_nn(f_im, c_im), dot_nn(f_re, c_im) + dot_nn(f_im, c_re)

    progress(8)
    finish(5)
    loads[1].wait()

    @pl.loop(0, 8)
    def _(m):
        rows = pl.ds(pl.multiple_of(m * 128, 128), 128)
        acc[0, rows, :], acc[1, rows, :] = outer(x, rows)

    start_back(7, batches[7])
    start_relay(6, batches[6])
    finish(6)

    @pl.loop(0, 8)
    def _(m):
        rows = pl.ds(pl.multiple_of(m * 128, 128), 128)
        left_re, left_im = outer(left, rows)
        right_re, right_im = outer(right, rows)
        acc[0, rows, :] += left_re + right_re
        acc[1, rows, :] += left_im + right_im

    start_relay(7, batches[7])
    finish(7)

    @pl.loop(0, 8)
    def _(m):
        rows = pl.ds(pl.multiple_of(m * 128, 128), 128)
        far_re, far_im = outer(far_x, rows)
        outer_re = acc[0, rows, :] + far_re
        outer_im = acc[1, rows, :] + far_im
        co, si = cosine[rows, :], sine[rows, :]
        dense_re[rows, :] = (outer_re * co + outer_im * si).astype(jnp.bfloat16)
        dense_im[rows, :] = (outer_im * co - outer_re * si).astype(jnp.bfloat16)


    half = RANK

    def z_half(h, sign):
        return dot_nn(qt[h], dense_re[...]) + sign * dot_nn(qt[1 - h], dense_im[...])

    sign = (1 - 2 * core).astype(jnp.float32)
    zs1[...] = z_half(other, -sign).astype(jnp.bfloat16)
    swap = remote(zs1, zr1, sz1, rz1, z * 2 + other, c)
    swap.start()
    zown[...] = z_half(core, sign)
    swap.wait_recv()
    mine = zown[...] + zr1[...].astype(jnp.float32)
    quarter = half // 4
    zs2[...] = mine.reshape(4, quarter, -1).astype(zs2.dtype)
    zown[...] = mine
    sends = []
    for d in range(1, 4):
        to = (z + d) % 4
        sends.append(remote(zs2.at[to], zr2.at[d - 1], sz2.at[d - 1], rz2.at[d - 1], to * 2 + core, c))
        sends[-1].start()
    total = zown[pl.ds(z * quarter, quarter), :]
    for d in range(1, 4):
        sends[d - 1].wait_recv()
        total = total + zr2[d - 1].astype(jnp.float32)
    slot = core * half + z * quarter
    own = zfull.at[pl.ds(slot, quarter), :]
    zfull[pl.ds(slot, quarter), :] = total.astype(jnp.bfloat16)
    spread = []
    for d in range(1, 4):
        to = (z + d) % 4
        spread.append(remote(own, own, sz3.at[d - 1], rz3.at[d - 1], to * 2 + core, c))
        spread[-1].start()
    hand = [remote(own, own, sz4.at[0], rz4.at[0], z * 2 + other, c)]
    hand[0].start()
    for d in range(1, 4):
        spread[d - 1].wait_recv()
        origin = (z + 4 - d) % 4
        part = zfull.at[pl.ds(core * half + origin * quarter, quarter), :]
        hand.append(remote(part, part, sz4.at[d], rz4.at[d], z * 2 + other, c))
        hand[-1].start()
    for d in range(4):
        hand[d].wait_recv()

    z_re, z_im = zfull.at[pl.ds(0, half), :], zfull.at[pl.ds(half, half), :]
    first_a, first_b = {}, {}
    for d in (2, 1, 3, 0):
        to = (x + d) % 4
        rows = pl.ds(to * 256, 256)
        block = (dot_nt(dense_re[rows, :], z_re[...]) - dot_nt(dense_im[rows, :], z_im[...])).reshape(4, 64, half)
        if d:
            ysa[d - 1] = block.astype(ysa.dtype)
            first_a[d] = remote(ysa.at[d - 1], yra.at[d - 1], sya.at[d - 1], rya.at[d - 1], r, to * 4 + y)
            first_a[d].start()
        else:
            yown_a[...] = block
        to = (y + d) % 4
        rows_re = jnp.concatenate([dense_re[pl.ds(i * 256 + to * 64, 64), :] for i in range(4)], axis=0)
        rows_im = jnp.concatenate([dense_im[pl.ds(i * 256 + to * 64, 64), :] for i in range(4)], axis=0)
        block = (dot_nt(rows_re, z_im[...]) + dot_nt(rows_im, z_re[...])).reshape(4, 64, half)
        if d:
            ysb[d - 1] = block.astype(ysb.dtype)
            first_b[d] = remote(ysb.at[d - 1], yrb.at[d - 1], syb.at[d - 1], ryb.at[d - 1], r, x * 4 + to)
            first_b[d].start()
        else:
            yown_b[...] = block
    sum_a = yown_a[...]
    for d in range(1, 4):
        first_a[d].wait_recv()
        sum_a = sum_a + yra[d - 1].astype(jnp.float32)
    yown_a[...] = sum_a
    ys2[0] = sum_a.astype(ys2.dtype)
    second_a = []
    for d in range(1, 4):
        to = (y + d) % 4
        second_a.append(remote(ys2.at[0, to], yr2a.at[d - 1], sy2a.at[d - 1], ry2a.at[d - 1], r, x * 4 + to))
        second_a[-1].start()
    sum_b = yown_b[...]
    for d in range(1, 4):
        first_b[d].wait_recv()
        sum_b = sum_b + yrb[d - 1].astype(jnp.float32)
    yown_b[...] = sum_b
    ys2[1] = sum_b.astype(ys2.dtype)
    second_b = []
    for d in range(1, 4):
        to = (x + d) % 4
        second_b.append(remote(ys2.at[1, to], yr2b.at[d - 1], sy2b.at[d - 1], ry2b.at[d - 1], r, to * 4 + y))
        second_b[-1].start()
    final_a = yown_a[y]
    for d in range(1, 4):
        second_a[d - 1].wait_recv()
        final_a = final_a + yr2a[d - 1].astype(jnp.float32)
    final_b = yown_b[x]
    for d in range(1, 4):
        second_b[d - 1].wait_recv()
        final_b = final_b + yr2b[d - 1].astype(jnp.float32)
    image_ref[:, :half] = final_a
    image_ref[:, half:] = final_b

    both = jnp.concatenate([final_a, final_b], axis=0)
    turned = jnp.concatenate([final_b, -final_a], axis=0)
    gram_re = dot_tn(both, both, HI)
    gram_im = dot_tn(both, turned, HI)
    rows = lax.broadcasted_iota(jnp.int32, (RANK, RANK), 0)
    cols = lax.broadcasted_iota(jnp.int32, (RANK, RANK), 1)
    hpart[...] = jnp.where(rows >= cols, gram_re, gram_im).reshape(16, 16, RANK)
    steps = sorted(((i, j) for i in range(4) for j in range(4) if i or j), key=lambda p: -min(p[0], 4 - p[0]) - min(p[1], 4 - p[1]))
    columns = [(x + i) % 4 * 4 + (y + j) % 4 for i, j in steps]
    g1 = []
    for d in range(1, 16):
        to = columns[d - 1]
        g1.append(remote(hpart.at[to], hrecv.at[d - 1], sh1.at[d - 1], rh1.at[d - 1], r, to))
        g1[-1].start()
    acc = hpart[c]
    for d in range(1, 16):
        g1[d - 1].wait_recv()
        acc = acc + hrecv[d - 1]
    hrow[r] = acc
    g2 = []
    for d in range(1, 8):
        g2.append(remote(hrow.at[r], hrow.at[r], sh2.at[d - 1], rh2.at[d - 1], (r + d) % 8, c))
        g2[-1].start()
    for d in range(1, 8):
        g2[d - 1].wait_recv()
    acc = hrow[0]
    for i in range(1, 8):
        acc = acc + hrow[i]
    gram_ref[c] = acc
    g3 = []
    for d in range(1, 16):
        g3.append(remote(gram_ref.at[c], gram_ref.at[c], sh3.at[d - 1], rh3.at[d - 1], r, columns[d - 1]))
        g3[-1].start()
    for d in range(1, 16):
        g3[d - 1].wait_recv()
    for copy in list(copies.values()) + [pair[s] for s in range(8)]:
        copy.wait_send()
    for s in range(8):
        for copy in across[s] + back[s] + relay[s]:
            copy.wait_send()
    for copy in [swap] + sends + spread + hand + list(first_a.values()) + list(first_b.values()) + second_a + second_b + g1 + g2 + g3:
        copy.wait_send()


def front(reflection, order, q, focus_in, focus_out, ref_angle):
    bf, f32 = jnp.bfloat16, jnp.float32
    vm, dma = pltpu.VMEM, pltpu.SemaphoreType.DMA
    vmem = pl.BlockSpec(memory_space=pltpu.VMEM)
    anywhere = pl.BlockSpec(memory_space=pl.ANY)
    scratch = [
        vm((4, 4, 2, 64, 2048), bf), vm((2, 2048, 512), bf), vm((2, 1024, 1024), bf), vm((1024, 512), f32), vm((1024, 512), f32),
        vm((8, 2, 4, 32, 512), f32), vm((8, 4, 32, 512), f32), vm((8, 4, 32, 512), f32), vm((8, 3, 32, 512), f32), vm((2, 1024, 512), bf),
        vm((4, 32, 512), bf), vm((4, 32, 512), bf), vm((4, 32, 512), bf), vm((3, 32, 512), bf),
        vm((2, 1024, 512), f32), vm((1024, 512), bf), vm((1024, 512), bf),
        vm((2, RANK, 1024), bf), vm((256, 512), f32), vm((256, 512), bf), vm((256, 512), bf), vm((4, 64, 512), bf), vm((3, 64, 512), bf), vm((512, 512), bf),
        vm((4, 64, 256), f32), vm((4, 64, 256), f32), vm((3, 4, 64, 256), bf), vm((3, 4, 64, 256), bf),
        vm((3, 4, 64, 256), bf), vm((3, 4, 64, 256), bf), vm((2, 4, 64, 256), bf), vm((3, 64, 256), bf), vm((3, 64, 256), bf),
        vm((16, 16, RANK), f32), vm((15, 16, RANK), f32), vm((8, 16, RANK), f32),
        dma((3,)), dma((40,)), dma((40,)), dma((8,)), dma((8,)), dma((8, 3)), dma((8, 3)), dma((8, 3)), dma((8, 3)), dma((8, 4)), dma((8, 4)),
        dma, dma, dma((3,)), dma((3,)), dma((3,)), dma((3,)), dma((4,)), dma((4,)), dma((3,)), dma((3,)), dma((3,)), dma((3,)),
        dma((3,)), dma((3,)), dma((3,)), dma((3,)), dma((15,)), dma((15,)), dma((7,)), dma((7,)), dma((15,)), dma((15,)),
    ]
    return pl.pallas_call(
        front_kernel,
        out_shape=(jax.ShapeDtypeStruct((64, 2 * RANK), f32), jax.ShapeDtypeStruct((16, 16, RANK), f32)),
        in_specs=[vmem, vmem, vmem, anywhere, anywhere, anywhere],
        out_specs=(vmem, vmem),
        scratch_shapes=scratch,
        compiler_params=pltpu.CompilerParams(collective_id=0, has_side_effects=True, vmem_limit_bytes=62 << 20),
    )(reflection, order, q, focus_in, focus_out, ref_angle)


def column(m, j):
    return jnp.broadcast_to(m[:, j : j + 1], m.shape)


def times_i_rows(m):
    return jnp.concatenate([-m[:, NB : 2 * NB], m[:, :NB], -m[:, 3 * NB :], m[:, 2 * NB : 3 * NB]], axis=1)


def factor_inverse(diag):
    lane = lax.broadcasted_iota(jnp.int32, (NB, 4 * NB), 1)
    sub = lax.broadcasted_iota(jnp.int32, (NB, 4 * NB), 0)
    w = jnp.concatenate([diag, jnp.zeros_like(diag)], axis=1) + (lane - 2 * NB == sub).astype(jnp.float32)
    row = lax.broadcasted_iota(jnp.int32, (8, 4 * NB), 0)
    done = []
    for base in range(0, NB, 8):
        top, under = w[:8], w[8:]
        more = under.shape[0] > 0
        turn = times_i_rows(top)
        cols = [(column(w, base + j), column(w, NB + base + j)) for j in range(8)]
        for j in range(0, 8, 2):
            (a_re, a_im), (b_re, b_im) = cols[j : j + 2]
            p, q = a_re[j : j + 1], b_re[j + 1 : j + 2]
            s_re, s_im = a_re[j + 1 : j + 2], a_im[j + 1 : j + 2]
            det = 1.0 / (p * q - (s_re * s_re + s_im * s_im))
            pd, qd, sd_re, sd_im = p * det, q * det, s_re * det, s_im * det
            for m in range(j + 2, 8):
                c_re, c_im = cols[m]
                x_re, x_im, y_re, y_im = c_re[j : j + 1], c_im[j : j + 1], c_re[j + 1 : j + 2], c_im[j + 1 : j + 2]
                g_re = qd * x_re - (sd_re * y_re + sd_im * y_im)
                g_im = qd * x_im - (sd_re * y_im - sd_im * y_re)
                h_re = pd * y_re - (sd_re * x_re - sd_im * x_im)
                h_im = pd * y_im - (sd_re * x_im + sd_im * x_re)
                cols[m] = (
                    c_re - ((a_re * g_re - a_im * g_im) + (b_re * h_re - b_im * h_im)),
                    c_im - ((a_re * g_im + a_im * g_re) + (b_re * h_im + b_im * h_re)),
                )
            w0, v0, w1, v1 = top[j : j + 1], turn[j : j + 1], top[j + 1 : j + 2], turn[j + 1 : j + 2]
            u0 = qd * w0 - (sd_re * w1 - sd_im * v1)
            t0 = qd * v0 - (sd_re * v1 + sd_im * w1)
            u1 = pd * w1 - (sd_re * w0 + sd_im * v0)
            t1 = pd * v1 - (sd_re * v0 - sd_im * w0)
            inv = 1.0 / p
            x0, y0 = (s_re * w0 + s_im * v0) * inv, (s_re * v0 - s_im * w0) * inv
            if more:
                d_re, d_im, e_re, e_im = a_re[8:], a_im[8:], b_re[8:], b_im[8:]
                under = under - ((d_re * u0 + d_im * t0) + (e_re * u1 + e_im * t1))
            d_re, d_im, e_re, e_im = a_re[:8], a_im[:8], b_re[:8], b_im[:8]
            dw = (d_re * u0 + d_im * t0) + (e_re * u1 + e_im * t1)
            dv = (d_re * t0 - d_im * u0) + (e_re * t1 - e_im * u1)
            top = top - jnp.where(row > j + 1, dw, jnp.where(row == j + 1, x0, 0.0))
            turn = turn - jnp.where(row > j + 1, dv, jnp.where(row == j + 1, y0, 0.0))
        d = jnp.sum(jnp.where(lane[:8] == row + base, top, 0.0), axis=1, keepdims=True)
        done.append(top[:, 2 * NB :] * lax.rsqrt(d))
        w = under
    return jnp.concatenate(done, axis=0)


def swapped(m):
    return jnp.concatenate([-m[:, NB:], m[:, :NB]], axis=1)


def chol_kernel(scale, g_ref, y_ref, out_ref, a_ref):
    n = RANK
    rows = y_ref.shape[0]
    panels = n // NB
    packed = g_ref[...]
    turned = packed.T
    sub = lax.broadcasted_iota(jnp.int32, (n, n), 0)
    lane = lax.broadcasted_iota(jnp.int32, (n, n), 1)
    g_re = jnp.where(sub >= lane, packed, turned)
    g_im = jnp.where(sub > lane, -turned, jnp.where(sub == lane, 0.0, packed))
    for k in range(panels):
        a_ref[:n, 2 * NB * k : 2 * NB * k + NB] = g_re[:, NB * k : NB * k + NB]
        a_ref[:n, 2 * NB * k + NB : 2 * NB * (k + 1)] = g_im[:, NB * k : NB * k + NB]
        a_ref[n:, 2 * NB * k : 2 * NB * k + NB] = y_ref[:, NB * k : NB * k + NB]
        a_ref[n:, 2 * NB * k + NB : 2 * NB * (k + 1)] = y_ref[:, n + NB * k : n + NB * k + NB]
    diag = a_ref[:NB, : 2 * NB]
    for k in range(panels):
        lo = k * NB
        inv = factor_inverse(diag)
        both = jnp.concatenate([inv, swapped(inv)], axis=0)
        left = panels - 1 - k
        if left:
            nxt = dot_nt(a_ref[lo + NB : lo + 2 * NB, 2 * lo : 2 * lo + 2 * NB], both, HI)
            turn = jnp.concatenate([nxt, swapped(nxt)], axis=0)
            diag = a_ref[lo + NB : lo + 2 * NB, 2 * lo + 2 * NB : 2 * lo + 4 * NB] - dot_nt(nxt, turn, HI)
        low = dot_nt(a_ref[lo + NB :, 2 * lo : 2 * lo + 2 * NB], both, HI)
        solved = low[low.shape[0] - rows :] * scale
        out_ref[:, 0, lo : lo + NB] = solved[:, :NB]
        out_ref[:, 1, lo : lo + NB] = solved[:, NB:]
        if left:
            lk = low[: left * NB]
            q = jnp.concatenate([lk.reshape(left, NB, 2 * NB), swapped(lk).reshape(left, NB, 2 * NB)], axis=1)
            q = q.reshape(left * 2 * NB, 2 * NB)
            a_ref[lo + NB :, 2 * lo + 2 * NB :] -= dot_nt(low, q, HI)


def chol(g, y, scale):
    vmem = pl.BlockSpec(memory_space=pltpu.VMEM)
    return pl.pallas_call(
        functools.partial(chol_kernel, scale),
        out_shape=jax.ShapeDtypeStruct((y.shape[0], 2, RANK), jnp.float32),
        in_specs=[vmem] * 2,
        out_specs=vmem,
        scratch_shapes=[pltpu.VMEM((RANK + y.shape[0], 2 * RANK), jnp.float32)],
    )(g, y)


def body(reflection, focus_in, focus_out, ref_angle, element_order, q_start):
    image, gram = front(reflection, element_order.reshape(1, -1), q_start, focus_in, focus_out, ref_angle)
    return chol(gram.reshape(RANK, RANK), image, math.sqrt(NF))


def solution(mesh):
    in_specs = (
        P(None, "col", "row"),
        P(None, "row", "col"),
        P(None, "row", None),
        P("row", "col"),
        P("row"),
        P("row", None, None),
    )
    out_specs = P(("row", "col"), None, None)
    return jax.shard_map(body, mesh=mesh, in_specs=in_specs, out_specs=out_specs, check_vma=False)
```

```python
import functools
import math

import jax
import jax.numpy as jnp
from jax import lax
from jax.experimental import pallas as pl
from jax.experimental.pallas import tpu as pltpu
from jax.sharding import PartitionSpec as P

NF = 8192
RANK = 256
PANEL_W = 512
NB = 64
HI = lax.Precision.HIGHEST
MESH = pl.DeviceIdType.MESH


def dot_nt(a, b, precision=None):
    return lax.dot_general(a, b, (((1,), (1,)), ((), ())), precision=precision, preferred_element_type=jnp.float32)


def dot_nn(a, b):
    return jnp.dot(a, b, preferred_element_type=jnp.float32)


def dot_tn(a, b, precision=None):
    return lax.dot_general(a, b, (((0,), (0,)), ((), ())), precision=precision, preferred_element_type=jnp.float32)


def remote(src, dst, send_sem, recv_sem, row, col):
    return pltpu.make_async_remote_copy(
        src_ref=src, dst_ref=dst, send_sem=send_sem, recv_sem=recv_sem, device_id=(row, col), device_id_type=MESH
    )


def cos_sin(angle):
    half = 0.5 * angle
    t = half * half
    s = -1.0 / 39916800.0
    for k in (1.0 / 362880.0, -1.0 / 5040.0, 1.0 / 120.0, -1.0 / 6.0, 1.0):
        s = s * t + k
    s = s * half
    c = 1.0 / 479001600.0
    for k in (-1.0 / 3628800.0, 1.0 / 40320.0, -1.0 / 720.0, 1.0 / 24.0, -0.5, 1.0):
        c = c * t + k
    return 1.0 - 2.0 * s * s, 2.0 * s * c


def front_kernel(
    refl_ref, order_ref, q_ref, focus_in_hbm, focus_out_hbm, angle_hbm, image_ref, gram_ref,
    gat, p_ref, f_ref, cosine, sine, cpart, crecv, zsend, zrecv, cfull, last_pair, last_recv, last_send, last_across, acc, dense_re, dense_im,
    qt, zown, zs1, zr1, zs2, zr2, zfull,
    yown_a, yown_b, ysa, ysb, yra, yrb, ys2, yr2a, yr2b,
    hpart, hrecv, hrow,
    local_sem, gs, gr, ps, pr, zs, zr, cs, cr, ws, wr,
    sz1, rz1, sz2, rz2, sz3, rz3, sz4, rz4, sya, rya, syb, ryb, sy2a, ry2a, sy2b, ry2b, sh1, rh1, sh2, rh2, sh3, rh3,
):
    r = lax.axis_index("row")
    c = lax.axis_index("col")
    z, core = r // 2, r % 2
    x, y = c // 4, c % 4
    other = 1 - core
    up = {"x": (x + 1) % 4, "y": (y + 1) % 4}
    down = {"x": (x + 3) % 4, "y": (y + 3) % 4}
    far_x, far_y = (x + 2) % 4, (y + 2) % 4
    left, right, low, high = down["x"], up["x"], down["y"], up["y"]

    loads = [
        pltpu.make_async_copy(focus_in_hbm, p_ref, local_sem.at[0]),
        pltpu.make_async_copy(focus_out_hbm, f_ref, local_sem.at[1]),
        pltpu.make_async_copy(angle_hbm, cosine, local_sem.at[2]),
    ]
    for copy in loads:
        copy.start()
    barrier = pltpu.get_barrier_semaphore()
    for d in range(1, 8):
        pl.semaphore_signal(barrier, inc=1, device_id=((r + d) % 8, c), device_id_type=MESH)
    for d in range(1, 16):
        pl.semaphore_signal(barrier, inc=1, device_id=(r, (c + d) % 16), device_id_type=MESH)

    sub = lax.broadcasted_iota(jnp.int32, (PANEL_W, PANEL_W), 0)
    for b in range(refl_ref.shape[2] // PANEL_W):
        lanes = pl.ds(b * PANEL_W, PANEL_W)
        place = order_ref[:, lanes] & (PANEL_W - 1)
        onehot = jnp.where(place == sub, 1.0, 0.0).astype(jnp.bfloat16)
        raw = jnp.concatenate([refl_ref[0, :32, lanes], refl_ref[1, :32, lanes], refl_ref[0, 32:, lanes], refl_ref[1, 32:, lanes]], axis=0)
        moved = dot_nt(raw, onehot).astype(jnp.bfloat16)
        gat[x, y, 0, :, lanes] = moved[:64]
        gat[x, y, 1, :, lanes] = moved[64:]
    pl.semaphore_wait(barrier, 22)

    copies = {}

    def send(name, sx, sy, h, piece=None):
        axis, way = name[-2], name[-1]
        to = (up if way == "+" else down)[axis]
        col = to * 4 + y if axis == "x" else x * 4 + to
        ref = gat.at[sx, sy, h] if piece is None else gat.at[sx, sy, h, pl.ds(32 * piece, 32)]
        i = len(copies)
        copies[name] = remote(ref, ref, gs.at[i], gr.at[i], r, col)
        copies[name].start()

    def got(*names):
        for name in names:
            copies[name + "+"].wait_recv()
            copies[name + "-"].wait_recv()

    def both(name, sx, sy, h):
        send(name + "+", sx, sy, h)
        send(name + "-", sx, sy, h)

    def gemm(s, parts):
        @pl.loop(0, 2)
        def _(n):
            lanes = pl.ds(pl.multiple_of(n * 256, 256), 256)
            rows = jnp.concatenate([gat[sx, sy, h] for sx, sy, h in parts], axis=0)
            by_re = dot_nn(rows, p_ref[0, :, lanes]).reshape(4, 2, 32, 256)
            by_im = dot_nn(rows, p_ref[1, :, lanes]).reshape(4, 2, 32, 256)
            cpart[s, 0, :, :, lanes] = by_re[:, 0] - by_im[:, 1]
            cpart[s, 1, :, :, lanes] = by_im[:, 0] + by_re[:, 1]

    pair, across, back, relay = {}, {}, {}, {}

    def start_pair(s):
        if s == 7:
            last_pair[...] = cpart[s, other].astype(jnp.bfloat16)
            pair[s] = remote(last_pair, last_recv, ps.at[s], pr.at[s], z * 2 + other, c)
        else:
            pair[s] = remote(cpart.at[s, other], crecv.at[s], ps.at[s], pr.at[s], z * 2 + other, c)
        pair[s].start()

    def start_across(s):
        pair[s].wait_recv()
        across[s] = []
        if s == 7:
            mine = cpart[s, core] + last_recv[...].astype(jnp.float32)
            last_send[...] = mine.astype(jnp.bfloat16)
        else:
            mine = cpart[s, core] + crecv[s]
        zsend[s] = mine
        for d in range(1, 4):
            to = (z + d) % 4
            if s == 7:
                src, dst = last_send.at[to], last_across.at[d - 1]
            else:
                src, dst = zsend.at[s, to], zrecv.at[s, d - 1]
            across[s].append(remote(src, dst, zs.at[s, d - 1], zr.at[s, d - 1], to * 2 + core, c))
            across[s][-1].start()

    def place_of(parts, q):
        first = jnp.int32(0)
        for i, (sx, sy, h) in enumerate(parts):
            first = first + jnp.where(q == i, 1, 0) * (sx * 256 + sy * 64 + h * 32)
        return pl.multiple_of(first, 32)

    def start_back(s, parts):
        total = zsend[s, z]
        for d in range(1, 4):
            across[s][d - 1].wait_recv()
            total = total + (last_across[d - 1].astype(jnp.float32) if s == 7 else zrecv[s, d - 1])
        mine = pl.ds(place_of(parts, z), 32)
        cfull[core, mine, :] = total.astype(jnp.bfloat16)
        ref = cfull.at[core, mine, :]
        back[s] = []
        for d in range(1, 4):
            back[s].append(remote(ref, ref, cs.at[s, d - 1], cr.at[s, d - 1], (z + d) % 4 * 2 + core, c))
            back[s][-1].start()
        relay[s] = [remote(ref, ref, ws.at[s, 0], wr.at[s, 0], z * 2 + other, c)]
        relay[s][0].start()

    def start_relay(s, parts):
        for d in range(1, 4):
            back[s][d - 1].wait_recv()
            ref = cfull.at[core, pl.ds(place_of(parts, (z + 4 - d) % 4), 32), :]
            relay[s].append(remote(ref, ref, ws.at[s, d], wr.at[s, d], z * 2 + other, c))
            relay[s][-1].start()

    def finish(s):
        for copy in relay[s]:
            copy.wait_recv()

    batches = [
        [(x, y, 0), (x, y, 1), (left, y, 0), (right, y, 0)],
        [(x, low, 1), (x, high, 1), (x, low, 0), (x, high, 0)],
        [(left, y, 1), (right, y, 1), (x, far_y, 1), (far_x, y, 0)],
        [(left, low, 0), (left, high, 0), (left, low, 1), (right, low, 1)],
        [(right, low, 0), (right, high, 0), (left, high, 1), (right, high, 1)],
        [(x, far_y, 0), (far_x, y, 1), (far_x, low, 0), (far_x, high, 0)],
        [(left, far_y, 1), (right, far_y, 1), (left, far_y, 0), (right, far_y, 0)],
        [(far_x, low, 1), (far_x, high, 1), (far_x, far_y, 0), (far_x, far_y, 1)],
    ]

    def progress(s):
        if 0 <= s - 1 < 8:
            start_across(s - 1)
        if 0 <= s - 2 < 8:
            start_back(s - 2, batches[s - 2])
        if 0 <= s - 3 < 8:
            start_relay(s - 3, batches[s - 3])
        if 0 <= s - 4 < 8:
            finish(s - 4)

    both("Ax", x, y, 0)
    both("By", x, y, 1)
    both("Ay", x, y, 0)
    both("Bx", x, y, 1)
    loads[0].wait()
    for s in range(8):
        if s == 0:
            got("Ax")
            send("Aqx+", left, y, 0, 0)
            send("Aqx-", right, y, 0, 1)
            got("By")
            send("Bqy+", x, low, 1, 0)
            send("Bqy-", x, high, 1, 1)
            both("A1y", left, y, 0)
            both("B1x", x, low, 1)
            both("A2y", right, y, 0)
            both("B2x", x, high, 1)
        elif s == 1:
            got("Ay")
            send("Aq0y+", x, low, 0, 0)
            send("Aq0y-", x, high, 0, 1)
            got("Bx")
            send("Bq0x+", left, y, 1, 0)
            send("Bq0x-", right, y, 1, 1)
        elif s == 2:
            got("Aqx")
            both("A3y", far_x, y, 0)
            got("Bqy")
            both("B3x", x, far_y, 1)
        elif s == 3:
            got("A1y")
            send("Aq1y+", left, low, 0, 0)
            send("Aq1y-", left, high, 0, 1)
            got("B1x")
            send("Bq1x+", left, low, 1, 0)
            send("Bq1x-", right, low, 1, 1)
        elif s == 4:
            got("A2y")
            send("Aq2y+", right, low, 0, 0)
            send("Aq2y-", right, high, 0, 1)
            got("B2x")
            send("Bq2x+", left, high, 1, 0)
            send("Bq2x-", right, high, 1, 1)
        elif s == 5:
            got("Aq0y", "Bq0x", "A3y")
            send("Aq3y+", far_x, low, 0, 0)
            send("Aq3y-", far_x, high, 0, 1)
            got("B3x")
            send("Bq3x+", left, far_y, 1, 0)
            send("Bq3x-", right, far_y, 1, 1)
        elif s == 6:
            got("Aq1y", "Aq2y")
        else:
            got("Bq1x", "Bq2x", "Aq3y", "Bq3x")
        progress(s)
        gemm(s, batches[s])
        start_pair(s)
        if s == 2:
            loads[2].wait()

            @pl.loop(0, 8)
            def _(m):
                rows = pl.ds(pl.multiple_of(m * 128, 128), 128)
                cosine[rows, :], sine[rows, :] = cos_sin(cosine[rows, :])
        if s == 3:
            qt[0] = q_ref[:, 0, :].T
            qt[1] = q_ref[:, 1, :].T

    def outer(to, rows):
        lanes = pl.ds(pl.multiple_of(to * 256, 256), 256)
        f_re, f_im = f_ref[0, rows, lanes], f_ref[1, rows, lanes]
        c_re, c_im = cfull[0, lanes, :], cfull[1, lanes, :]
        return dot_nn(f_re, c_re) - dot_nn(f_im, c_im), dot_nn(f_re, c_im) + dot_nn(f_im, c_re)

    progress(8)
    finish(5)
    loads[1].wait()

    @pl.loop(0, 8)
    def _(m):
        rows = pl.ds(pl.multiple_of(m * 128, 128), 128)
        acc[0, rows, :], acc[1, rows, :] = outer(x, rows)

    start_back(7, batches[7])
    start_relay(6, batches[6])
    finish(6)

    @pl.loop(0, 8)
    def _(m):
        rows = pl.ds(pl.multiple_of(m * 128, 128), 128)
        left_re, left_im = outer(left, rows)
        right_re, right_im = outer(right, rows)
        acc[0, rows, :] += left_re + right_re
        acc[1, rows, :] += left_im + right_im

    start_relay(7, batches[7])
    finish(7)

    @pl.loop(0, 8)
    def _(m):
        rows = pl.ds(pl.multiple_of(m * 128, 128), 128)
        far_re, far_im = outer(far_x, rows)
        outer_re = acc[0, rows, :] + far_re
        outer_im = acc[1, rows, :] + far_im
        co, si = cosine[rows, :], sine[rows, :]
        dense_re[rows, :] = (outer_re * co + outer_im * si).astype(jnp.bfloat16)
        dense_im[rows, :] = (outer_im * co - outer_re * si).astype(jnp.bfloat16)


    half = RANK

    def z_half(h, sign):
        return dot_nn(qt[h], dense_re[...]) + sign * dot_nn(qt[1 - h], dense_im[...])

    sign = (1 - 2 * core).astype(jnp.float32)
    zs1[...] = z_half(other, -sign).astype(jnp.bfloat16)
    eighth = half // 8
    swap, sends, spread, hand = [], [], [], []
    for g in range(2):
        part = pl.ds(g * 4 * eighth, 4 * eighth)
        swap.append(remote(zs1.at[part, :], zr1.at[part, :], sz1.at[g], rz1.at[g], z * 2 + other, c))
        swap[g].start()
    zown[...] = z_half(core, sign)
    for g in range(2):
        part = pl.ds(g * 4 * eighth, 4 * eighth)
        swap[g].wait_recv()
        mine = zown[part, :] + zr1[part, :].astype(jnp.float32)
        zs2[g] = mine.reshape(4, eighth, -1).astype(zs2.dtype)
        zown[part, :] = mine
        for d in range(1, 4):
            to = (z + d) % 4
            sends.append(remote(zs2.at[g, to], zr2.at[g, d - 1], sz2.at[g, d - 1], rz2.at[g, d - 1], to * 2 + core, c))
            sends[-1].start()
    for g in range(2):
        total = zown[pl.ds((g * 4 + z) * eighth, eighth), :]
        for d in range(1, 4):
            sends[3 * g + d - 1].wait_recv()
            total = total + zr2[g, d - 1].astype(jnp.float32)
        slot = core * half + (g * 4 + z) * eighth
        zfull[pl.ds(slot, eighth), :] = total.astype(jnp.bfloat16)
        own = zfull.at[pl.ds(slot, eighth), :]
        for d in range(1, 4):
            spread.append(remote(own, own, sz3.at[g, d - 1], rz3.at[g, d - 1], (z + d) % 4 * 2 + core, c))
            spread[-1].start()
        hand.append(remote(own, own, sz4.at[g, 0], rz4.at[g, 0], z * 2 + other, c))
        hand[-1].start()
    for g in range(2):
        for d in range(1, 4):
            spread[3 * g + d - 1].wait_recv()
            part = zfull.at[pl.ds(core * half + (g * 4 + (z + 4 - d) % 4) * eighth, eighth), :]
            hand.append(remote(part, part, sz4.at[g, d], rz4.at[g, d], z * 2 + other, c))
            hand[-1].start()
    for copy in hand:
        copy.wait_recv()

    z_re, z_im = zfull.at[pl.ds(0, half), :], zfull.at[pl.ds(half, half), :]
    first_a, first_b = {}, {}
    for d in (2, 1, 3, 0):
        to = (x + d) % 4
        rows = pl.ds(to * 256, 256)
        block = (dot_nt(dense_re[rows, :], z_re[...]) - dot_nt(dense_im[rows, :], z_im[...])).reshape(4, 64, half)
        if d:
            ysa[d - 1] = block.astype(ysa.dtype)
            first_a[d] = remote(ysa.at[d - 1], yra.at[d - 1], sya.at[d - 1], rya.at[d - 1], r, to * 4 + y)
            first_a[d].start()
        else:
            yown_a[...] = block
        to = (y + d) % 4
        rows_re = jnp.concatenate([dense_re[pl.ds(i * 256 + to * 64, 64), :] for i in range(4)], axis=0)
        rows_im = jnp.concatenate([dense_im[pl.ds(i * 256 + to * 64, 64), :] for i in range(4)], axis=0)
        block = (dot_nt(rows_re, z_im[...]) + dot_nt(rows_im, z_re[...])).reshape(4, 64, half)
        if d:
            ysb[d - 1] = block.astype(ysb.dtype)
            first_b[d] = remote(ysb.at[d - 1], yrb.at[d - 1], syb.at[d - 1], ryb.at[d - 1], r, x * 4 + to)
            first_b[d].start()
        else:
            yown_b[...] = block
    sum_a = yown_a[...]
    for d in range(1, 4):
        first_a[d].wait_recv()
        sum_a = sum_a + yra[d - 1].astype(jnp.float32)
    yown_a[...] = sum_a
    ys2[0] = sum_a.astype(ys2.dtype)
    second_a = []
    for d in range(1, 4):
        to = (y + d) % 4
        second_a.append(remote(ys2.at[0, to], yr2a.at[d - 1], sy2a.at[d - 1], ry2a.at[d - 1], r, x * 4 + to))
        second_a[-1].start()
    sum_b = yown_b[...]
    for d in range(1, 4):
        first_b[d].wait_recv()
        sum_b = sum_b + yrb[d - 1].astype(jnp.float32)
    yown_b[...] = sum_b
    ys2[1] = sum_b.astype(ys2.dtype)
    second_b = []
    for d in range(1, 4):
        to = (x + d) % 4
        second_b.append(remote(ys2.at[1, to], yr2b.at[d - 1], sy2b.at[d - 1], ry2b.at[d - 1], r, to * 4 + y))
        second_b[-1].start()
    final_a = yown_a[y]
    for d in range(1, 4):
        second_a[d - 1].wait_recv()
        final_a = final_a + yr2a[d - 1].astype(jnp.float32)
    final_b = yown_b[x]
    for d in range(1, 4):
        second_b[d - 1].wait_recv()
        final_b = final_b + yr2b[d - 1].astype(jnp.float32)
    image_ref[:, :half] = final_a
    image_ref[:, half:] = final_b

    both = jnp.concatenate([final_a, final_b], axis=0)
    turned = jnp.concatenate([final_b, -final_a], axis=0)
    gram_re = dot_tn(both, both, HI)
    gram_im = dot_tn(both, turned, HI)
    rows = lax.broadcasted_iota(jnp.int32, (RANK, RANK), 0)
    cols = lax.broadcasted_iota(jnp.int32, (RANK, RANK), 1)
    hpart[...] = jnp.where(rows >= cols, gram_re, gram_im).reshape(16, 16, RANK)
    steps = sorted(((i, j) for i in range(4) for j in range(4) if i or j), key=lambda p: -min(p[0], 4 - p[0]) - min(p[1], 4 - p[1]))
    columns = [(x + i) % 4 * 4 + (y + j) % 4 for i, j in steps]
    g1 = []
    for d in range(1, 16):
        to = columns[d - 1]
        g1.append(remote(hpart.at[to], hrecv.at[d - 1], sh1.at[d - 1], rh1.at[d - 1], r, to))
        g1[-1].start()
    acc = hpart[c]
    for d in range(1, 16):
        g1[d - 1].wait_recv()
        acc = acc + hrecv[d - 1]
    hrow[r] = acc
    g2 = []
    for d in range(1, 8):
        g2.append(remote(hrow.at[r], hrow.at[r], sh2.at[d - 1], rh2.at[d - 1], (r + d) % 8, c))
        g2[-1].start()
    for d in range(1, 8):
        g2[d - 1].wait_recv()
    acc = hrow[0]
    for i in range(1, 8):
        acc = acc + hrow[i]
    gram_ref[c] = acc
    g3 = []
    for d in range(1, 16):
        g3.append(remote(gram_ref.at[c], gram_ref.at[c], sh3.at[d - 1], rh3.at[d - 1], r, columns[d - 1]))
        g3[-1].start()
    for d in range(1, 16):
        g3[d - 1].wait_recv()
    for copy in list(copies.values()) + [pair[s] for s in range(8)]:
        copy.wait_send()
    for s in range(8):
        for copy in across[s] + back[s] + relay[s]:
            copy.wait_send()
    for copy in swap + sends + spread + hand + list(first_a.values()) + list(first_b.values()) + second_a + second_b + g1 + g2 + g3:
        copy.wait_send()


def front(reflection, order, q, focus_in, focus_out, ref_angle):
    bf, f32 = jnp.bfloat16, jnp.float32
    vm, dma = pltpu.VMEM, pltpu.SemaphoreType.DMA
    vmem = pl.BlockSpec(memory_space=pltpu.VMEM)
    anywhere = pl.BlockSpec(memory_space=pl.ANY)
    scratch = [
        vm((4, 4, 2, 64, 2048), bf), vm((2, 2048, 512), bf), vm((2, 1024, 1024), bf), vm((1024, 512), f32), vm((1024, 512), f32),
        vm((8, 2, 4, 32, 512), f32), vm((8, 4, 32, 512), f32), vm((8, 4, 32, 512), f32), vm((8, 3, 32, 512), f32), vm((2, 1024, 512), bf),
        vm((4, 32, 512), bf), vm((4, 32, 512), bf), vm((4, 32, 512), bf), vm((3, 32, 512), bf),
        vm((2, 1024, 512), f32), vm((1024, 512), bf), vm((1024, 512), bf),
        vm((2, RANK, 1024), bf), vm((256, 512), f32), vm((256, 512), bf), vm((256, 512), bf), vm((2, 4, 32, 512), bf), vm((2, 3, 32, 512), bf), vm((512, 512), bf),
        vm((4, 64, 256), f32), vm((4, 64, 256), f32), vm((3, 4, 64, 256), bf), vm((3, 4, 64, 256), bf),
        vm((3, 4, 64, 256), bf), vm((3, 4, 64, 256), bf), vm((2, 4, 64, 256), bf), vm((3, 64, 256), bf), vm((3, 64, 256), bf),
        vm((16, 16, RANK), f32), vm((15, 16, RANK), f32), vm((8, 16, RANK), f32),
        dma((3,)), dma((40,)), dma((40,)), dma((8,)), dma((8,)), dma((8, 3)), dma((8, 3)), dma((8, 3)), dma((8, 3)), dma((8, 4)), dma((8, 4)),
        dma((2,)), dma((2,)), dma((2, 3)), dma((2, 3)), dma((2, 3)), dma((2, 3)), dma((2, 4)), dma((2, 4)), dma((3,)), dma((3,)), dma((3,)), dma((3,)),
        dma((3,)), dma((3,)), dma((3,)), dma((3,)), dma((15,)), dma((15,)), dma((7,)), dma((7,)), dma((15,)), dma((15,)),
    ]
    return pl.pallas_call(
        front_kernel,
        out_shape=(jax.ShapeDtypeStruct((64, 2 * RANK), f32), jax.ShapeDtypeStruct((16, 16, RANK), f32)),
        in_specs=[vmem, vmem, vmem, anywhere, anywhere, anywhere],
        out_specs=(vmem, vmem),
        scratch_shapes=scratch,
        compiler_params=pltpu.CompilerParams(collective_id=0, has_side_effects=True, vmem_limit_bytes=62 << 20),
    )(reflection, order, q, focus_in, focus_out, ref_angle)


def column(m, j):
    return jnp.broadcast_to(m[:, j : j + 1], m.shape)


def times_i_rows(m):
    return jnp.concatenate([-m[:, NB : 2 * NB], m[:, :NB], -m[:, 3 * NB :], m[:, 2 * NB : 3 * NB]], axis=1)


def factor_inverse(diag):
    lane = lax.broadcasted_iota(jnp.int32, (NB, 4 * NB), 1)
    sub = lax.broadcasted_iota(jnp.int32, (NB, 4 * NB), 0)
    w = jnp.concatenate([diag, jnp.zeros_like(diag)], axis=1) + (lane - 2 * NB == sub).astype(jnp.float32)
    row = lax.broadcasted_iota(jnp.int32, (8, 4 * NB), 0)
    done = []
    for base in range(0, NB, 8):
        top, under = w[:8], w[8:]
        more = under.shape[0] > 0
        turn = times_i_rows(top)
        cols = [(column(w, base + j), column(w, NB + base + j)) for j in range(8)]
        for j in range(0, 8, 2):
            (a_re, a_im), (b_re, b_im) = cols[j : j + 2]
            p, q = a_re[j : j + 1], b_re[j + 1 : j + 2]
            s_re, s_im = a_re[j + 1 : j + 2], a_im[j + 1 : j + 2]
            det = 1.0 / (p * q - (s_re * s_re + s_im * s_im))
            pd, qd, sd_re, sd_im = p * det, q * det, s_re * det, s_im * det
            for m in range(j + 2, 8):
                c_re, c_im = cols[m]
                x_re, x_im, y_re, y_im = c_re[j : j + 1], c_im[j : j + 1], c_re[j + 1 : j + 2], c_im[j + 1 : j + 2]
                g_re = qd * x_re - (sd_re * y_re + sd_im * y_im)
                g_im = qd * x_im - (sd_re * y_im - sd_im * y_re)
                h_re = pd * y_re - (sd_re * x_re - sd_im * x_im)
                h_im = pd * y_im - (sd_re * x_im + sd_im * x_re)
                cols[m] = (
                    c_re - ((a_re * g_re - a_im * g_im) + (b_re * h_re - b_im * h_im)),
                    c_im - ((a_re * g_im + a_im * g_re) + (b_re * h_im + b_im * h_re)),
                )
            w0, v0, w1, v1 = top[j : j + 1], turn[j : j + 1], top[j + 1 : j + 2], turn[j + 1 : j + 2]
            u0 = qd * w0 - (sd_re * w1 - sd_im * v1)
            t0 = qd * v0 - (sd_re * v1 + sd_im * w1)
            u1 = pd * w1 - (sd_re * w0 + sd_im * v0)
            t1 = pd * v1 - (sd_re * v0 - sd_im * w0)
            inv = 1.0 / p
            x0, y0 = (s_re * w0 + s_im * v0) * inv, (s_re * v0 - s_im * w0) * inv
            if more:
                d_re, d_im, e_re, e_im = a_re[8:], a_im[8:], b_re[8:], b_im[8:]
                under = under - ((d_re * u0 + d_im * t0) + (e_re * u1 + e_im * t1))
            d_re, d_im, e_re, e_im = a_re[:8], a_im[:8], b_re[:8], b_im[:8]
            dw = (d_re * u0 + d_im * t0) + (e_re * u1 + e_im * t1)
            dv = (d_re * t0 - d_im * u0) + (e_re * t1 - e_im * u1)
            top = top - jnp.where(row > j + 1, dw, jnp.where(row == j + 1, x0, 0.0))
            turn = turn - jnp.where(row > j + 1, dv, jnp.where(row == j + 1, y0, 0.0))
        d = jnp.sum(jnp.where(lane[:8] == row + base, top, 0.0), axis=1, keepdims=True)
        done.append(top[:, 2 * NB :] * lax.rsqrt(d))
        w = under
    return jnp.concatenate(done, axis=0)


def swapped(m):
    return jnp.concatenate([-m[:, NB:], m[:, :NB]], axis=1)


def chol_kernel(scale, g_ref, y_ref, out_ref, a_ref):
    n = RANK
    rows = y_ref.shape[0]
    panels = n // NB
    packed = g_ref[...]
    turned = packed.T
    sub = lax.broadcasted_iota(jnp.int32, (n, n), 0)
    lane = lax.broadcasted_iota(jnp.int32, (n, n), 1)
    g_re = jnp.where(sub >= lane, packed, turned)
    g_im = jnp.where(sub > lane, -turned, jnp.where(sub == lane, 0.0, packed))
    for k in range(panels):
        a_ref[:n, 2 * NB * k : 2 * NB * k + NB] = g_re[:, NB * k : NB * k + NB]
        a_ref[:n, 2 * NB * k + NB : 2 * NB * (k + 1)] = g_im[:, NB * k : NB * k + NB]
        a_ref[n:, 2 * NB * k : 2 * NB * k + NB] = y_ref[:, NB * k : NB * k + NB]
        a_ref[n:, 2 * NB * k + NB : 2 * NB * (k + 1)] = y_ref[:, n + NB * k : n + NB * k + NB]
    diag = a_ref[:NB, : 2 * NB]
    for k in range(panels):
        lo = k * NB
        inv = factor_inverse(diag)
        both = jnp.concatenate([inv, swapped(inv)], axis=0)
        left = panels - 1 - k
        if left:
            nxt = dot_nt(a_ref[lo + NB : lo + 2 * NB, 2 * lo : 2 * lo + 2 * NB], both, HI)
            turn = jnp.concatenate([nxt, swapped(nxt)], axis=0)
            diag = a_ref[lo + NB : lo + 2 * NB, 2 * lo + 2 * NB : 2 * lo + 4 * NB] - dot_nt(nxt, turn, HI)
        low = dot_nt(a_ref[lo + NB :, 2 * lo : 2 * lo + 2 * NB], both, HI)
        solved = low[low.shape[0] - rows :] * scale
        out_ref[:, 0, lo : lo + NB] = solved[:, :NB]
        out_ref[:, 1, lo : lo + NB] = solved[:, NB:]
        if left:
            lk = low[: left * NB]
            q = jnp.concatenate([lk.reshape(left, NB, 2 * NB), swapped(lk).reshape(left, NB, 2 * NB)], axis=1)
            q = q.reshape(left * 2 * NB, 2 * NB)
            a_ref[lo + NB :, 2 * lo + 2 * NB :] -= dot_nt(low, q, HI)


def chol(g, y, scale):
    vmem = pl.BlockSpec(memory_space=pltpu.VMEM)
    return pl.pallas_call(
        functools.partial(chol_kernel, scale),
        out_shape=jax.ShapeDtypeStruct((y.shape[0], 2, RANK), jnp.float32),
        in_specs=[vmem] * 2,
        out_specs=vmem,
        scratch_shapes=[pltpu.VMEM((RANK + y.shape[0], 2 * RANK), jnp.float32)],
    )(g, y)


def body(reflection, focus_in, focus_out, ref_angle, element_order, q_start):
    image, gram = front(reflection, element_order.reshape(1, -1), q_start, focus_in, focus_out, ref_angle)
    return chol(gram.reshape(RANK, RANK), image, math.sqrt(NF))


def solution(mesh):
    in_specs = (
        P(None, "col", "row"),
        P(None, "row", "col"),
        P(None, "row", None),
        P("row", "col"),
        P("row"),
        P("row", None, None),
    )
    out_specs = P(("row", "col"), None, None)
    return jax.shard_map(body, mesh=mesh, in_specs=in_specs, out_specs=out_specs, check_vma=False)
```

```python
import functools
import math

import jax
import jax.numpy as jnp
from jax import lax
from jax.experimental import pallas as pl
from jax.experimental.pallas import tpu as pltpu
from jax.sharding import PartitionSpec as P

NF = 8192
RANK = 256
PANEL_W = 512
NB = 64
HI = lax.Precision.HIGHEST
MESH = pl.DeviceIdType.MESH


def dot_nt(a, b, precision=None):
    return lax.dot_general(a, b, (((1,), (1,)), ((), ())), precision=precision, preferred_element_type=jnp.float32)


def dot_nn(a, b):
    return jnp.dot(a, b, preferred_element_type=jnp.float32)


def dot_tn(a, b, precision=None):
    return lax.dot_general(a, b, (((0,), (0,)), ((), ())), precision=precision, preferred_element_type=jnp.float32)


def remote(src, dst, send_sem, recv_sem, row, col):
    return pltpu.make_async_remote_copy(
        src_ref=src, dst_ref=dst, send_sem=send_sem, recv_sem=recv_sem, device_id=(row, col), device_id_type=MESH
    )


def cos_sin(angle):
    half = 0.5 * angle
    t = half * half
    s = -1.0 / 39916800.0
    for k in (1.0 / 362880.0, -1.0 / 5040.0, 1.0 / 120.0, -1.0 / 6.0, 1.0):
        s = s * t + k
    s = s * half
    c = 1.0 / 479001600.0
    for k in (-1.0 / 3628800.0, 1.0 / 40320.0, -1.0 / 720.0, 1.0 / 24.0, -0.5, 1.0):
        c = c * t + k
    return 1.0 - 2.0 * s * s, 2.0 * s * c


def front_kernel(
    refl_ref, order_ref, q_ref, focus_in_hbm, focus_out_hbm, angle_hbm, image_ref, gram_ref,
    gat, p_ref, f_ref, cosine, sine, cpart, crecv, zsend, zrecv, cfull, last_pair, last_recv, last_send, last_across, acc, dense_re, dense_im,
    qt, zown, zs1, zr1, zs2, zr2, zfull,
    yown_a, yown_b, ysa, ysb, yra, yrb, ys2, yr2a, yr2b,
    hpart, hrecv, hrow,
    local_sem, gs, gr, ps, pr, zs, zr, cs, cr, ws, wr,
    sz1, rz1, sz2, rz2, sz3, rz3, sz4, rz4, sya, rya, syb, ryb, sy2a, ry2a, sy2b, ry2b, sh1, rh1, sh2, rh2, sh3, rh3,
):
    r = lax.axis_index("row")
    c = lax.axis_index("col")
    z, core = r // 2, r % 2
    x, y = c // 4, c % 4
    other = 1 - core
    up = {"x": (x + 1) % 4, "y": (y + 1) % 4}
    down = {"x": (x + 3) % 4, "y": (y + 3) % 4}
    far_x, far_y = (x + 2) % 4, (y + 2) % 4
    left, right, low, high = down["x"], up["x"], down["y"], up["y"]

    loads = [
        pltpu.make_async_copy(focus_in_hbm, p_ref, local_sem.at[0]),
        pltpu.make_async_copy(focus_out_hbm, f_ref, local_sem.at[1]),
        pltpu.make_async_copy(angle_hbm, cosine, local_sem.at[2]),
    ]
    for copy in loads:
        copy.start()
    barrier = pltpu.get_barrier_semaphore()
    for d in range(1, 8):
        pl.semaphore_signal(barrier, inc=1, device_id=((r + d) % 8, c), device_id_type=MESH)
    for d in range(1, 16):
        pl.semaphore_signal(barrier, inc=1, device_id=(r, (c + d) % 16), device_id_type=MESH)

    sub = lax.broadcasted_iota(jnp.int32, (PANEL_W, PANEL_W), 0)
    for b in range(refl_ref.shape[2] // PANEL_W):
        lanes = pl.ds(b * PANEL_W, PANEL_W)
        place = order_ref[:, lanes] & (PANEL_W - 1)
        onehot = jnp.where(place == sub, 1.0, 0.0).astype(jnp.bfloat16)
        raw = jnp.concatenate([refl_ref[0, :32, lanes], refl_ref[1, :32, lanes], refl_ref[0, 32:, lanes], refl_ref[1, 32:, lanes]], axis=0)
        moved = dot_nt(raw, onehot).astype(jnp.bfloat16)
        gat[x, y, 0, :, lanes] = moved[:64]
        gat[x, y, 1, :, lanes] = moved[64:]
    pl.semaphore_wait(barrier, 22)

    copies = {}

    def send(name, sx, sy, h, piece=None):
        axis, way = name[-2], name[-1]
        to = (up if way == "+" else down)[axis]
        col = to * 4 + y if axis == "x" else x * 4 + to
        ref = gat.at[sx, sy, h] if piece is None else gat.at[sx, sy, h, pl.ds(32 * piece, 32)]
        i = len(copies)
        copies[name] = remote(ref, ref, gs.at[i], gr.at[i], r, col)
        copies[name].start()

    def got(*names):
        for name in names:
            copies[name + "+"].wait_recv()
            copies[name + "-"].wait_recv()

    def both(name, sx, sy, h):
        send(name + "+", sx, sy, h)
        send(name + "-", sx, sy, h)

    def gemm(s, parts):
        @pl.loop(0, 2)
        def _(n):
            lanes = pl.ds(pl.multiple_of(n * 256, 256), 256)
            rows = jnp.concatenate([gat[sx, sy, h] for sx, sy, h in parts], axis=0)
            by_re = dot_nn(rows, p_ref[0, :, lanes]).reshape(4, 2, 32, 256)
            by_im = dot_nn(rows, p_ref[1, :, lanes]).reshape(4, 2, 32, 256)
            cpart[s, 0, :, :, lanes] = by_re[:, 0] - by_im[:, 1]
            cpart[s, 1, :, :, lanes] = by_im[:, 0] + by_re[:, 1]

    pair, across, back, relay = {}, {}, {}, {}

    def start_pair(s):
        if s == 7:
            last_pair[...] = cpart[s, other].astype(jnp.bfloat16)
            pair[s] = remote(last_pair, last_recv, ps.at[s], pr.at[s], z * 2 + other, c)
        else:
            pair[s] = remote(cpart.at[s, other], crecv.at[s], ps.at[s], pr.at[s], z * 2 + other, c)
        pair[s].start()

    def start_across(s):
        pair[s].wait_recv()
        across[s] = []
        if s == 7:
            mine = cpart[s, core] + last_recv[...].astype(jnp.float32)
            last_send[...] = mine.astype(jnp.bfloat16)
        else:
            mine = cpart[s, core] + crecv[s]
        zsend[s] = mine
        for d in range(1, 4):
            to = (z + d) % 4
            if s == 7:
                src, dst = last_send.at[to], last_across.at[d - 1]
            else:
                src, dst = zsend.at[s, to], zrecv.at[s, d - 1]
            across[s].append(remote(src, dst, zs.at[s, d - 1], zr.at[s, d - 1], to * 2 + core, c))
            across[s][-1].start()

    def place_of(parts, q):
        first = jnp.int32(0)
        for i, (sx, sy, h) in enumerate(parts):
            first = first + jnp.where(q == i, 1, 0) * (sx * 256 + sy * 64 + h * 32)
        return pl.multiple_of(first, 32)

    def start_back(s, parts):
        total = zsend[s, z]
        for d in range(1, 4):
            across[s][d - 1].wait_recv()
            total = total + (last_across[d - 1].astype(jnp.float32) if s == 7 else zrecv[s, d - 1])
        mine = pl.ds(place_of(parts, z), 32)
        cfull[core, mine, :] = total.astype(jnp.bfloat16)
        ref = cfull.at[core, mine, :]
        back[s] = []
        for d in range(1, 4):
            back[s].append(remote(ref, ref, cs.at[s, d - 1], cr.at[s, d - 1], (z + d) % 4 * 2 + core, c))
            back[s][-1].start()
        relay[s] = [remote(ref, ref, ws.at[s, 0], wr.at[s, 0], z * 2 + other, c)]
        relay[s][0].start()

    def start_relay(s, parts):
        for d in range(1, 4):
            back[s][d - 1].wait_recv()
            ref = cfull.at[core, pl.ds(place_of(parts, (z + 4 - d) % 4), 32), :]
            relay[s].append(remote(ref, ref, ws.at[s, d], wr.at[s, d], z * 2 + other, c))
            relay[s][-1].start()

    def finish(s):
        for copy in relay[s]:
            copy.wait_recv()

    batches = [
        [(x, y, 0), (x, y, 1), (left, y, 0), (right, y, 0)],
        [(x, low, 1), (x, high, 1), (x, low, 0), (x, high, 0)],
        [(left, y, 1), (right, y, 1), (x, far_y, 1), (far_x, y, 0)],
        [(left, low, 0), (left, high, 0), (left, low, 1), (right, low, 1)],
        [(right, low, 0), (right, high, 0), (left, high, 1), (right, high, 1)],
        [(x, far_y, 0), (far_x, y, 1), (far_x, low, 0), (far_x, high, 0)],
        [(left, far_y, 1), (right, far_y, 1), (left, far_y, 0), (right, far_y, 0)],
        [(far_x, low, 1), (far_x, high, 1), (far_x, far_y, 0), (far_x, far_y, 1)],
    ]

    def progress(s):
        if 0 <= s - 1 < 8:
            start_across(s - 1)
        if 0 <= s - 2 < 8:
            start_back(s - 2, batches[s - 2])
        if 0 <= s - 3 < 8:
            start_relay(s - 3, batches[s - 3])
        if 0 <= s - 4 < 8:
            finish(s - 4)

    both("Ax", x, y, 0)
    both("By", x, y, 1)
    both("Ay", x, y, 0)
    both("Bx", x, y, 1)
    loads[0].wait()
    for s in range(8):
        if s == 0:
            got("Ax")
            send("Aqx+", left, y, 0, 0)
            send("Aqx-", right, y, 0, 1)
            got("By")
            send("Bqy+", x, low, 1, 0)
            send("Bqy-", x, high, 1, 1)
            both("A1y", left, y, 0)
            both("B1x", x, low, 1)
            both("A2y", right, y, 0)
            both("B2x", x, high, 1)
        elif s == 1:
            got("Ay")
            send("Aq0y+", x, low, 0, 0)
            send("Aq0y-", x, high, 0, 1)
            got("Bx")
            send("Bq0x+", left, y, 1, 0)
            send("Bq0x-", right, y, 1, 1)
        elif s == 2:
            got("Aqx")
            both("A3y", far_x, y, 0)
            got("Bqy")
            both("B3x", x, far_y, 1)
        elif s == 3:
            got("A1y")
            send("Aq1y+", left, low, 0, 0)
            send("Aq1y-", left, high, 0, 1)
            got("B1x")
            send("Bq1x+", left, low, 1, 0)
            send("Bq1x-", right, low, 1, 1)
        elif s == 4:
            got("A2y")
            send("Aq2y+", right, low, 0, 0)
            send("Aq2y-", right, high, 0, 1)
            got("B2x")
            send("Bq2x+", left, high, 1, 0)
            send("Bq2x-", right, high, 1, 1)
        elif s == 5:
            got("Aq0y", "Bq0x", "A3y")
            send("Aq3y+", far_x, low, 0, 0)
            send("Aq3y-", far_x, high, 0, 1)
            got("B3x")
            send("Bq3x+", left, far_y, 1, 0)
            send("Bq3x-", right, far_y, 1, 1)
        elif s == 6:
            got("Aq1y", "Aq2y")
        else:
            got("Bq1x", "Bq2x", "Aq3y", "Bq3x")
        progress(s)
        gemm(s, batches[s])
        start_pair(s)
        if s == 2:
            loads[2].wait()

            @pl.loop(0, 8)
            def _(m):
                rows = pl.ds(pl.multiple_of(m * 128, 128), 128)
                cosine[rows, :], sine[rows, :] = cos_sin(cosine[rows, :])
        if s == 3:
            qt[0] = q_ref[:, 0, :].T
            qt[1] = q_ref[:, 1, :].T

    def outer(to, rows):
        lanes = pl.ds(pl.multiple_of(to * 256, 256), 256)
        f_re, f_im = f_ref[0, rows, lanes], f_ref[1, rows, lanes]
        c_re, c_im = cfull[0, lanes, :], cfull[1, lanes, :]
        return dot_nn(f_re, c_re) - dot_nn(f_im, c_im), dot_nn(f_re, c_im) + dot_nn(f_im, c_re)

    progress(8)
    finish(5)
    loads[1].wait()

    @pl.loop(0, 8)
    def _(m):
        rows = pl.ds(pl.multiple_of(m * 128, 128), 128)
        acc[0, rows, :], acc[1, rows, :] = outer(x, rows)

    start_back(7, batches[7])
    start_relay(6, batches[6])
    finish(6)

    @pl.loop(0, 8)
    def _(m):
        rows = pl.ds(pl.multiple_of(m * 128, 128), 128)
        left_re, left_im = outer(left, rows)
        right_re, right_im = outer(right, rows)
        acc[0, rows, :] += left_re + right_re
        acc[1, rows, :] += left_im + right_im

    start_relay(7, batches[7])
    finish(7)

    @pl.loop(0, 8)
    def _(m):
        rows = pl.ds(pl.multiple_of(m * 128, 128), 128)
        far_re, far_im = outer(far_x, rows)
        outer_re = acc[0, rows, :] + far_re
        outer_im = acc[1, rows, :] + far_im
        co, si = cosine[rows, :], sine[rows, :]
        dense_re[rows, :] = (outer_re * co + outer_im * si).astype(jnp.bfloat16)
        dense_im[rows, :] = (outer_im * co - outer_re * si).astype(jnp.bfloat16)


    half = RANK

    def z_half(h, sign):
        return dot_nn(qt[h], dense_re[...]) + sign * dot_nn(qt[1 - h], dense_im[...])

    sign = (1 - 2 * core).astype(jnp.float32)
    zs1[...] = z_half(other, -sign).astype(jnp.bfloat16)
    eighth = half // 8
    swap, sends, spread, hand = [], [], [], []
    for g in range(2):
        part = pl.ds(g * 4 * eighth, 4 * eighth)
        swap.append(remote(zs1.at[part, :], zr1.at[part, :], sz1.at[g], rz1.at[g], z * 2 + other, c))
        swap[g].start()
    zown[...] = z_half(core, sign)
    for g in range(2):
        part = pl.ds(g * 4 * eighth, 4 * eighth)
        swap[g].wait_recv()
        mine = zown[part, :] + zr1[part, :].astype(jnp.float32)
        zs2[g] = mine.reshape(4, eighth, -1).astype(zs2.dtype)
        zown[part, :] = mine
        for d in range(1, 4):
            to = (z + d) % 4
            sends.append(remote(zs2.at[g, to], zr2.at[g, d - 1], sz2.at[g, d - 1], rz2.at[g, d - 1], to * 2 + core, c))
            sends[-1].start()
    for g in range(2):
        total = zown[pl.ds((g * 4 + z) * eighth, eighth), :]
        for d in range(1, 4):
            sends[3 * g + d - 1].wait_recv()
            total = total + zr2[g, d - 1].astype(jnp.float32)
        slot = core * half + (g * 4 + z) * eighth
        zfull[pl.ds(slot, eighth), :] = total.astype(jnp.bfloat16)
        own = zfull.at[pl.ds(slot, eighth), :]
        for d in range(1, 4):
            spread.append(remote(own, own, sz3.at[g, d - 1], rz3.at[g, d - 1], (z + d) % 4 * 2 + core, c))
            spread[-1].start()
        hand.append(remote(own, own, sz4.at[g, 0], rz4.at[g, 0], z * 2 + other, c))
        hand[-1].start()
    for g in range(2):
        for d in range(1, 4):
            spread[3 * g + d - 1].wait_recv()
            part = zfull.at[pl.ds(core * half + (g * 4 + (z + 4 - d) % 4) * eighth, eighth), :]
            hand.append(remote(part, part, sz4.at[g, d], rz4.at[g, d], z * 2 + other, c))
            hand[-1].start()
    for copy in hand:
        copy.wait_recv()

    z_re, z_im = zfull.at[pl.ds(0, half), :], zfull.at[pl.ds(half, half), :]
    first_a, first_b = {}, {}
    for d in (2, 1, 3, 0):
        to = (x + d) % 4
        rows = pl.ds(to * 256, 256)
        block = (dot_nt(dense_re[rows, :], z_re[...]) - dot_nt(dense_im[rows, :], z_im[...])).reshape(4, 64, half)
        if d:
            for p in range(2):
                ysa[p, d - 1] = block[:, :, p * 128 : p * 128 + 128].astype(ysa.dtype)
                first_a[d, p] = remote(ysa.at[p, d - 1], yra.at[p, d - 1], sya.at[p, d - 1], rya.at[p, d - 1], r, to * 4 + y)
                first_a[d, p].start()
        else:
            yown_a[...] = block
        to = (y + d) % 4
        rows_re = jnp.concatenate([dense_re[pl.ds(i * 256 + to * 64, 64), :] for i in range(4)], axis=0)
        rows_im = jnp.concatenate([dense_im[pl.ds(i * 256 + to * 64, 64), :] for i in range(4)], axis=0)
        block = (dot_nt(rows_re, z_im[...]) + dot_nt(rows_im, z_re[...])).reshape(4, 64, half)
        if d:
            for p in range(2):
                ysb[p, d - 1] = block[:, :, p * 128 : p * 128 + 128].astype(ysb.dtype)
                first_b[d, p] = remote(ysb.at[p, d - 1], yrb.at[p, d - 1], syb.at[p, d - 1], ryb.at[p, d - 1], r, x * 4 + to)
                first_b[d, p].start()
        else:
            yown_b[...] = block
    second_a, second_b = {}, {}
    for p in range(2):
        lanes = pl.ds(p * 128, 128)
        for k, own, first, got_ref, second, out_sem, in_sem, land in (
            (0, yown_a, first_a, yra, second_a, sy2a, ry2a, yr2a),
            (1, yown_b, first_b, yrb, second_b, sy2b, ry2b, yr2b),
        ):
            total = own[:, :, lanes]
            for d in range(1, 4):
                first[d, p].wait_recv()
                total = total + got_ref[p, d - 1].astype(jnp.float32)
            own[:, :, lanes] = total
            ys2[k, p] = total.astype(ys2.dtype)
            for d in range(1, 4):
                to = (y + d) % 4 if k == 0 else (x + d) % 4
                col = x * 4 + to if k == 0 else to * 4 + y
                second[d, p] = remote(ys2.at[k, p, to], land.at[p, d - 1], out_sem.at[p, d - 1], in_sem.at[p, d - 1], r, col)
                second[d, p].start()
    pieces_a, pieces_b = [], []
    for p in range(2):
        lanes = pl.ds(p * 128, 128)
        for pieces, own, mine, second, land in ((pieces_a, yown_a, y, second_a, yr2a), (pieces_b, yown_b, x, second_b, yr2b)):
            total = own[mine, :, lanes]
            for d in range(1, 4):
                second[d, p].wait_recv()
                total = total + land[p, d - 1].astype(jnp.float32)
            pieces.append(total)
    final_a = jnp.concatenate(pieces_a, axis=1)
    final_b = jnp.concatenate(pieces_b, axis=1)
    image_ref[:, :half] = final_a
    image_ref[:, half:] = final_b

    both = jnp.concatenate([final_a, final_b], axis=0)
    turned = jnp.concatenate([final_b, -final_a], axis=0)
    gram_re = dot_tn(both, both, HI)
    gram_im = dot_tn(both, turned, HI)
    rows = lax.broadcasted_iota(jnp.int32, (RANK, RANK), 0)
    cols = lax.broadcasted_iota(jnp.int32, (RANK, RANK), 1)
    hpart[...] = jnp.where(rows >= cols, gram_re, gram_im).reshape(16, 16, RANK)
    steps = sorted(((i, j) for i in range(4) for j in range(4) if i or j), key=lambda p: -min(p[0], 4 - p[0]) - min(p[1], 4 - p[1]))
    columns = [(x + i) % 4 * 4 + (y + j) % 4 for i, j in steps]
    g1 = []
    for d in range(1, 16):
        to = columns[d - 1]
        g1.append(remote(hpart.at[to], hrecv.at[d - 1], sh1.at[d - 1], rh1.at[d - 1], r, to))
        g1[-1].start()
    acc = hpart[c]
    for d in range(1, 16):
        g1[d - 1].wait_recv()
        acc = acc + hrecv[d - 1]
    hrow[r] = acc
    g2 = []
    for d in range(1, 8):
        g2.append(remote(hrow.at[r], hrow.at[r], sh2.at[d - 1], rh2.at[d - 1], (r + d) % 8, c))
        g2[-1].start()
    for d in range(1, 8):
        g2[d - 1].wait_recv()
    acc = hrow[0]
    for i in range(1, 8):
        acc = acc + hrow[i]
    gram_ref[c] = acc
    g3 = []
    for d in range(1, 16):
        g3.append(remote(gram_ref.at[c], gram_ref.at[c], sh3.at[d - 1], rh3.at[d - 1], r, columns[d - 1]))
        g3[-1].start()
    for d in range(1, 16):
        g3[d - 1].wait_recv()
    for copy in list(copies.values()) + [pair[s] for s in range(8)]:
        copy.wait_send()
    for s in range(8):
        for copy in across[s] + back[s] + relay[s]:
            copy.wait_send()
    for copy in swap + sends + spread + hand + list(first_a.values()) + list(first_b.values()) + list(second_a.values()) + list(second_b.values()) + g1 + g2 + g3:
        copy.wait_send()


def front(reflection, order, q, focus_in, focus_out, ref_angle):
    bf, f32 = jnp.bfloat16, jnp.float32
    vm, dma = pltpu.VMEM, pltpu.SemaphoreType.DMA
    vmem = pl.BlockSpec(memory_space=pltpu.VMEM)
    anywhere = pl.BlockSpec(memory_space=pl.ANY)
    scratch = [
        vm((4, 4, 2, 64, 2048), bf), vm((2, 2048, 512), bf), vm((2, 1024, 1024), bf), vm((1024, 512), f32), vm((1024, 512), f32),
        vm((8, 2, 4, 32, 512), f32), vm((8, 4, 32, 512), f32), vm((8, 4, 32, 512), f32), vm((8, 3, 32, 512), f32), vm((2, 1024, 512), bf),
        vm((4, 32, 512), bf), vm((4, 32, 512), bf), vm((4, 32, 512), bf), vm((3, 32, 512), bf),
        vm((2, 1024, 512), f32), vm((1024, 512), bf), vm((1024, 512), bf),
        vm((2, RANK, 1024), bf), vm((256, 512), f32), vm((256, 512), bf), vm((256, 512), bf), vm((2, 4, 32, 512), bf), vm((2, 3, 32, 512), bf), vm((512, 512), bf),
        vm((4, 64, 256), f32), vm((4, 64, 256), f32), vm((2, 3, 4, 64, 128), bf), vm((2, 3, 4, 64, 128), bf),
        vm((2, 3, 4, 64, 128), bf), vm((2, 3, 4, 64, 128), bf), vm((2, 2, 4, 64, 128), bf), vm((2, 3, 64, 128), bf), vm((2, 3, 64, 128), bf),
        vm((16, 16, RANK), f32), vm((15, 16, RANK), f32), vm((8, 16, RANK), f32),
        dma((3,)), dma((40,)), dma((40,)), dma((8,)), dma((8,)), dma((8, 3)), dma((8, 3)), dma((8, 3)), dma((8, 3)), dma((8, 4)), dma((8, 4)),
        dma((2,)), dma((2,)), dma((2, 3)), dma((2, 3)), dma((2, 3)), dma((2, 3)), dma((2, 4)), dma((2, 4)), dma((2, 3)), dma((2, 3)), dma((2, 3)), dma((2, 3)),
        dma((2, 3)), dma((2, 3)), dma((2, 3)), dma((2, 3)), dma((15,)), dma((15,)), dma((7,)), dma((7,)), dma((15,)), dma((15,)),
    ]
    return pl.pallas_call(
        front_kernel,
        out_shape=(jax.ShapeDtypeStruct((64, 2 * RANK), f32), jax.ShapeDtypeStruct((16, 16, RANK), f32)),
        in_specs=[vmem, vmem, vmem, anywhere, anywhere, anywhere],
        out_specs=(vmem, vmem),
        scratch_shapes=scratch,
        compiler_params=pltpu.CompilerParams(collective_id=0, has_side_effects=True, vmem_limit_bytes=62 << 20),
    )(reflection, order, q, focus_in, focus_out, ref_angle)


def column(m, j):
    return jnp.broadcast_to(m[:, j : j + 1], m.shape)


def times_i_rows(m):
    return jnp.concatenate([-m[:, NB : 2 * NB], m[:, :NB], -m[:, 3 * NB :], m[:, 2 * NB : 3 * NB]], axis=1)


def factor_inverse(diag):
    lane = lax.broadcasted_iota(jnp.int32, (NB, 4 * NB), 1)
    sub = lax.broadcasted_iota(jnp.int32, (NB, 4 * NB), 0)
    w = jnp.concatenate([diag, jnp.zeros_like(diag)], axis=1) + (lane - 2 * NB == sub).astype(jnp.float32)
    row = lax.broadcasted_iota(jnp.int32, (8, 4 * NB), 0)
    done = []
    for base in range(0, NB, 8):
        top, under = w[:8], w[8:]
        more = under.shape[0] > 0
        turn = times_i_rows(top)
        cols = [(column(w, base + j), column(w, NB + base + j)) for j in range(8)]
        for j in range(0, 8, 2):
            (a_re, a_im), (b_re, b_im) = cols[j : j + 2]
            p, q = a_re[j : j + 1], b_re[j + 1 : j + 2]
            s_re, s_im = a_re[j + 1 : j + 2], a_im[j + 1 : j + 2]
            det = 1.0 / (p * q - (s_re * s_re + s_im * s_im))
            pd, qd, sd_re, sd_im = p * det, q * det, s_re * det, s_im * det
            for m in range(j + 2, 8):
                c_re, c_im = cols[m]
                x_re, x_im, y_re, y_im = c_re[j : j + 1], c_im[j : j + 1], c_re[j + 1 : j + 2], c_im[j + 1 : j + 2]
                g_re = qd * x_re - (sd_re * y_re + sd_im * y_im)
                g_im = qd * x_im - (sd_re * y_im - sd_im * y_re)
                h_re = pd * y_re - (sd_re * x_re - sd_im * x_im)
                h_im = pd * y_im - (sd_re * x_im + sd_im * x_re)
                cols[m] = (
                    c_re - ((a_re * g_re - a_im * g_im) + (b_re * h_re - b_im * h_im)),
                    c_im - ((a_re * g_im + a_im * g_re) + (b_re * h_im + b_im * h_re)),
                )
            w0, v0, w1, v1 = top[j : j + 1], turn[j : j + 1], top[j + 1 : j + 2], turn[j + 1 : j + 2]
            u0 = qd * w0 - (sd_re * w1 - sd_im * v1)
            t0 = qd * v0 - (sd_re * v1 + sd_im * w1)
            u1 = pd * w1 - (sd_re * w0 + sd_im * v0)
            t1 = pd * v1 - (sd_re * v0 - sd_im * w0)
            inv = 1.0 / p
            x0, y0 = (s_re * w0 + s_im * v0) * inv, (s_re * v0 - s_im * w0) * inv
            if more:
                d_re, d_im, e_re, e_im = a_re[8:], a_im[8:], b_re[8:], b_im[8:]
                under = under - ((d_re * u0 + d_im * t0) + (e_re * u1 + e_im * t1))
            d_re, d_im, e_re, e_im = a_re[:8], a_im[:8], b_re[:8], b_im[:8]
            dw = (d_re * u0 + d_im * t0) + (e_re * u1 + e_im * t1)
            dv = (d_re * t0 - d_im * u0) + (e_re * t1 - e_im * u1)
            top = top - jnp.where(row > j + 1, dw, jnp.where(row == j + 1, x0, 0.0))
            turn = turn - jnp.where(row > j + 1, dv, jnp.where(row == j + 1, y0, 0.0))
        d = jnp.sum(jnp.where(lane[:8] == row + base, top, 0.0), axis=1, keepdims=True)
        done.append(top[:, 2 * NB :] * lax.rsqrt(d))
        w = under
    return jnp.concatenate(done, axis=0)


def swapped(m):
    return jnp.concatenate([-m[:, NB:], m[:, :NB]], axis=1)


def chol_kernel(scale, g_ref, y_ref, out_ref, a_ref):
    n = RANK
    rows = y_ref.shape[0]
    panels = n // NB
    packed = g_ref[...]
    turned = packed.T
    sub = lax.broadcasted_iota(jnp.int32, (n, n), 0)
    lane = lax.broadcasted_iota(jnp.int32, (n, n), 1)
    g_re = jnp.where(sub >= lane, packed, turned)
    g_im = jnp.where(sub > lane, -turned, jnp.where(sub == lane, 0.0, packed))
    for k in range(panels):
        a_ref[:n, 2 * NB * k : 2 * NB * k + NB] = g_re[:, NB * k : NB * k + NB]
        a_ref[:n, 2 * NB * k + NB : 2 * NB * (k + 1)] = g_im[:, NB * k : NB * k + NB]
        a_ref[n:, 2 * NB * k : 2 * NB * k + NB] = y_ref[:, NB * k : NB * k + NB]
        a_ref[n:, 2 * NB * k + NB : 2 * NB * (k + 1)] = y_ref[:, n + NB * k : n + NB * k + NB]
    diag = a_ref[:NB, : 2 * NB]
    for k in range(panels):
        lo = k * NB
        inv = factor_inverse(diag)
        both = jnp.concatenate([inv, swapped(inv)], axis=0)
        left = panels - 1 - k
        if left:
            nxt = dot_nt(a_ref[lo + NB : lo + 2 * NB, 2 * lo : 2 * lo + 2 * NB], both, HI)
            turn = jnp.concatenate([nxt, swapped(nxt)], axis=0)
            diag = a_ref[lo + NB : lo + 2 * NB, 2 * lo + 2 * NB : 2 * lo + 4 * NB] - dot_nt(nxt, turn, HI)
        low = dot_nt(a_ref[lo + NB :, 2 * lo : 2 * lo + 2 * NB], both, HI)
        solved = low[low.shape[0] - rows :] * scale
        out_ref[:, 0, lo : lo + NB] = solved[:, :NB]
        out_ref[:, 1, lo : lo + NB] = solved[:, NB:]
        if left:
            lk = low[: left * NB]
            q = jnp.concatenate([lk.reshape(left, NB, 2 * NB), swapped(lk).reshape(left, NB, 2 * NB)], axis=1)
            q = q.reshape(left * 2 * NB, 2 * NB)
            a_ref[lo + NB :, 2 * lo + 2 * NB :] -= dot_nt(low, q, HI)


def chol(g, y, scale):
    vmem = pl.BlockSpec(memory_space=pltpu.VMEM)
    return pl.pallas_call(
        functools.partial(chol_kernel, scale),
        out_shape=jax.ShapeDtypeStruct((y.shape[0], 2, RANK), jnp.float32),
        in_specs=[vmem] * 2,
        out_specs=vmem,
        scratch_shapes=[pltpu.VMEM((RANK + y.shape[0], 2 * RANK), jnp.float32)],
    )(g, y)


def body(reflection, focus_in, focus_out, ref_angle, element_order, q_start):
    image, gram = front(reflection, element_order.reshape(1, -1), q_start, focus_in, focus_out, ref_angle)
    return chol(gram.reshape(RANK, RANK), image, math.sqrt(NF))


def solution(mesh):
    in_specs = (
        P(None, "col", "row"),
        P(None, "row", "col"),
        P(None, "row", None),
        P("row", "col"),
        P("row"),
        P("row", None, None),
    )
    out_specs = P(("row", "col"), None, None)
    return jax.shard_map(body, mesh=mesh, in_specs=in_specs, out_specs=out_specs, check_vma=False)
```
